128 devices in a mesh: gx: 16 (over x, z), gy: 8 (over y, core).
Axes of the slice: x: 4, y: 4, z: 4, core: 2. Of those that a mesh axis runs over, the one named last changes fastest.
Arguments:
- states: bfloat16 [2, 64, 8, 128, 1024], P(None, None, None, 'gx', 'gy'), may hold values from -6 to 6, as said below
- class_map: int32 [8, 128, 1024], P(None, 'gx', 'gy'), may hold values from 0 to 7
- perm_table: float32 [8], replicated, may hold values from 0.05 to 1
- candidates: int32 [16, 8, 64], replicated, may hold values from 0 to 8191, as said below
- merge_order: int32 [127, 128], replicated, may hold values from 0 to 127, each once within a row
Outputs:
- flux: bfloat16 [64, 8, 128, 1024], P(None, None, 'gx', 'gy')
- kept_rows: float32 [127, 64, 64], replicated
The draws below stay inside these ranges and needn't reach their ends.
Inputs may be any that keep to these rules, and one draw needn't show every extreme that they name: states[0] is pressure; states[1] is water saturation, between 0.05 and 0.95. `candidates`: each tile's 64 entries are distinct cell numbers (z * 8 + x) * 128 + y of that tile's own cells. `merge_order`: each row is a permutation of 0 to 127.
All inputs are finite; a program needn't handle non-finite values.
Results may differ from the reference program's by a relative error of at most 0.001.
Values may be sent and summed in bfloat16 or wider, within the bound.
No kernel may reach another device: no remote copies, remote signals or barrier semaphores. Data moves between devices by JAX's collectives and lax.ppermute only.
A program may use at most 128 MiB of HBM per device.

```python
import math
import jax
import jax.numpy as jnp
from jax import lax

K = 64
NZW = 8
NCLASS = 8
CX = 8
CY = 128
NX = 128
NY = 1024
NODES = 127
N_GX = 16
N_GY = 8


def draw_states(key, part):
    key_p = jax.random.fold_in(key, 11)
    key_s = jax.random.fold_in(key, 12)
    shape = (K, NZW, NX, NY)
    pressure = jnp.clip(jax.random.normal(key_p, shape, jnp.float32), -6.0, 6.0)
    saturation = jax.random.uniform(key_s, shape, jnp.float32, 0.1, 0.9)
    return jnp.stack([pressure, saturation]).astype(jnp.bfloat16)


def draw_candidates(key, part):
    cell_count = NZW * CX * CY
    tile_keys = jax.random.split(jax.random.fold_in(key, 21), N_GX * N_GY)
    picked = jax.vmap(lambda one_key: jax.random.permutation(one_key, cell_count)[:K])(tile_keys)
    return picked.reshape(N_GX, N_GY, K).astype(jnp.int32)


def plant(drawn, rng, smallest, largest):
    shape = drawn.shape
    spot = [jax.random.randint(jax.random.fold_in(rng, axis), (), 0, shape[axis]) for axis in range(len(shape))]
    drawn = drawn.at[tuple(spot)].set(smallest)
    longest = shape.index(max(shape))
    spot[longest] = (spot[longest] + 1) % shape[longest]
    return drawn.at[tuple(spot)].set(largest)


def setup_inputs(seed: int = 0) -> dict:
    streams_of = jax.random.split(jax.random.key(seed), 6)
    states = draw_states(jax.random.fold_in(streams_of[5], 71), 0)
    class_map = plant(jax.random.randint(streams_of[1], (NZW, NX, NY), 0, NCLASS), jax.random.fold_in(streams_of[1], 1), 0, NCLASS - 1).astype(jnp.int32)
    perm_table = jnp.clip(jnp.exp(jax.random.uniform(streams_of[2], (NCLASS,), jnp.float32, math.log(0.05), math.log(1.0))), 0.05, 1.0)
    candidates = draw_candidates(jax.random.fold_in(streams_of[5], 71), 0)
    merge_order = jax.vmap(lambda own: jax.random.permutation(own, 2 * K))(jax.random.split(streams_of[4], NODES)).reshape((NODES, 2 * K)).astype(jnp.int32)
    return {"states": states, "class_map": class_map, "perm_table": perm_table, "candidates": candidates, "merge_order": merge_order}


def face_term(p_here, m_here, k_here, p_next, m_next, k_next):
    transmit = 2.0 * k_here * k_next / (k_here + k_next)
    return transmit * (0.5 * (m_here + m_next)) * (p_next - p_here)


def snapshot_flux(pressure, mobility, permeability):
    def rolled(offset_by, along):
        return face_term(pressure, mobility, permeability, jnp.roll(pressure, offset_by, along), jnp.roll(mobility, offset_by, along), jnp.roll(permeability, offset_by, along))

    summed = rolled(-1, 1) + rolled(1, 1)
    summed = summed + rolled(-1, 2)
    summed = summed + rolled(1, 2)
    upper_face = face_term(pressure[:-1], mobility[:-1], permeability[:-1], pressure[1:], mobility[1:], permeability[1:])
    lower_face = face_term(pressure[1:], mobility[1:], permeability[1:], pressure[:-1], mobility[:-1], permeability[:-1])
    zero_plane = jnp.zeros((1,) + pressure.shape[1:], jnp.float32)
    summed = summed + jnp.concatenate([upper_face, zero_plane], axis=0)
    summed = summed + jnp.concatenate([zero_plane, lower_face], axis=0)
    return summed


def tournament(cand_rows, merge_order):
    kept_count = merge_order.shape[1] // 2
    level_rows = cand_rows
    offset = 0
    kept_list = []
    for level_num in range(cand_rows.shape[0].bit_length() - 1):
        groups = level_rows.shape[0] // 2
        paired = level_rows.reshape((groups, 2 * kept_count) + level_rows.shape[2:])
        node_order = merge_order[offset:offset + groups, :kept_count]
        level_rows = jnp.take_along_axis(paired, node_order[:, :, None], axis=1)
        kept_list.append(level_rows)
        offset = offset + groups
    return jnp.concatenate(kept_list, axis=0)


def reference(states, class_map, perm_table, candidates, merge_order):
    permeability = perm_table[class_map]
    tile_area = CX * CY
    tile_x = jnp.arange(N_GX, dtype=jnp.int32)[:, None, None]
    tile_y = jnp.arange(N_GY, dtype=jnp.int32)[None, :, None]
    plane_idx = candidates // tile_area
    within = candidates % tile_area
    glob_x = tile_x * CX + within // CY
    glob_y = tile_y * CY + within % CY
    flat_index = ((plane_idx * NX + glob_x) * NY + glob_y).reshape(-1).astype(jnp.int32)

    def per_snapshot(index):
        snapshot = lax.dynamic_index_in_dim(states, index, 1, keepdims=False)
        pressure = snapshot[0].astype(jnp.float32)
        saturation = snapshot[1].astype(jnp.float32)
        summed = snapshot_flux(pressure, saturation * saturation, permeability)
        return summed.astype(jnp.bfloat16), summed.reshape(-1)[flat_index]

    flux, picked = lax.map(per_snapshot, jnp.arange(K, dtype=jnp.int32))
    cand_rows = jnp.transpose(picked).reshape(N_GX * N_GY, K, K)
    return flux, tournament(cand_rows, merge_order)
```

```python
import functools

import jax
import jax.numpy as jnp
from jax import lax
from jax.experimental import pallas as pl
from jax.experimental.pallas import tpu as pltpu
from jax.sharding import PartitionSpec as P

F32 = jnp.float32
BF16 = jnp.bfloat16
CHUNK = 16


def lane_of(shape):
    return lax.broadcasted_iota(jnp.int32, shape, len(shape) - 1)


def edge_kernel(states_ref, class_ref, low_ref, high_ref, side_ref, wide_ref, acc_ref):
    step = pl.program_id(0)
    chunk = states_ref.shape[1]
    snaps = chunk * pl.num_programs(0)
    base = step * chunk
    cells = 64

    @pl.when(step == 0)
    def _():
        acc_ref[...] = jnp.zeros_like(acc_ref)
        kind = class_ref[...].astype(F32)
        wide_ref[pl.ds(0, cells), :] = kind.reshape(cells, 128)
        low_ref[2 * 64] = wide_ref[pl.ds(0, 8, stride=8), :].astype(BF16)
        high_ref[2 * 64] = wide_ref[pl.ds(7, 8, stride=8), :].astype(BF16)
        first = jnp.broadcast_to(kind[:, :, 0:1], kind.shape)
        last = jnp.broadcast_to(kind[:, :, 127:128], kind.shape)
        even = lane_of(kind.shape) % 2 == 0
        side_ref[2] = jnp.where(even, first, last).astype(BF16)

    for field in range(2):
        acc = acc_ref[field]
        for k in range(chunk):
            value = states_ref[field, k].astype(F32).reshape(cells, 128)
            slot = (field * chunk + k) * cells
            wide_ref[pl.ds(slot, cells), :] = value
            place = 2 * (base + k)
            turned = pltpu.roll(value, place, 1)
            lane = lane_of(value.shape)
            acc = jnp.where((lane == place) | (lane == (place + 127) % 128), turned, acc)
            low_ref[field * 64 + base + k] = wide_ref[pl.ds(slot, 8, stride=8), :].astype(BF16)
            high_ref[field * 64 + base + k] = wide_ref[pl.ds(slot + 7, 8, stride=8), :].astype(BF16)
        acc_ref[field] = acc

    @pl.when(step == pl.num_programs(0) - 1)
    def _():
        side_ref[0] = acc_ref[0].reshape(8, 8, 128).astype(BF16)
        side_ref[1] = acc_ref[1].reshape(8, 8, 128).astype(BF16)


def look_up(kind, table_ref):
    value = jnp.zeros(kind.shape, F32)
    for number in range(8):
        value = jnp.where(kind == number, table_ref[number], value)
    return value


def trans(k_here, k_next):
    return k_here * k_next / (k_here + k_next)


def flux_kernel(
    table_ref, cand_ref, where_ref, states_ref, class_ref, low_ref, high_ref, side_ref,
    from_low_ref, from_high_ref, side_low_ref, side_high_ref,
    out_ref, rows_ref, flux_ref, tx_ref, ty_ref, tz_ref, txe_ref, qy_ref,
):
    step = pl.program_id(0)
    chunk = states_ref.shape[1]
    base = step * chunk
    shape = (8, 8, 128)

    @pl.when(step == 0)
    def _():
        perm = look_up(class_ref[...], table_ref)
        row = lax.broadcasted_iota(jnp.int32, shape, 1)
        lane = lane_of(shape)
        flat = perm.reshape(64, 128)
        next_x = jnp.roll(perm, -1, 1)
        next_y = pltpu.roll(flat, 127, 1).reshape(shape)
        tx_ref[...] = jnp.where(row == 7, 0.0, trans(perm, next_x))
        ty_ref[...] = jnp.where(lane == 127, 0.0, trans(perm, next_y))
        tz_ref[...] = trans(perm[:-1], perm[1:])
        k_low = look_up(low_ref[128].astype(F32), table_ref)
        k_high = look_up(high_ref[128].astype(F32), table_ref)
        txe_ref[0] = trans(k_low, look_up(from_low_ref[128].astype(F32), table_ref))
        txe_ref[1] = trans(k_high, look_up(from_high_ref[128].astype(F32), table_ref))
        even = lax.broadcasted_iota(jnp.int32, (64, 128), 1) % 2 == 0

        def beyond(which):
            below = side_low_ref[which].astype(F32).reshape(64, 128)
            above = side_high_ref[which].astype(F32).reshape(64, 128)
            return jnp.where(even, pltpu.roll(below, 1, 1), pltpu.roll(above, 127, 1))

        def here(which):
            return side_ref[which].astype(F32).reshape(64, 128)

        t_side = trans(look_up(here(2), table_ref), look_up(beyond(2), table_ref))
        s_here, s_next = here(1), beyond(1)
        qy_ref[...] = t_side * (s_here * s_here + s_next * s_next) * (beyond(0) - here(0))

    def face(t, l_here, l_next, p_here, p_next):
        return t * (l_here + l_next) * (p_next - p_here)

    lane = lax.broadcasted_iota(jnp.int32, (64, 128), 1)
    at_edge = (lane == 0) | (lane == 127)

    for k in range(chunk):
        snap = base + k
        p = states_ref[0, k].astype(F32)
        s = states_ref[1, k].astype(F32)
        m = s * s
        fx = face(tx_ref[...], m, jnp.roll(m, -1, 1), p, jnp.roll(p, -1, 1))
        total = fx - jnp.roll(fx, 1, 1)
        pf, mf = p.reshape(64, 128), m.reshape(64, 128)
        fy = face(
            ty_ref[...].reshape(64, 128), mf, pltpu.roll(mf, 127, 1), pf, pltpu.roll(pf, 127, 1)
        )
        total = total + (fy - pltpu.roll(fy, 1, 1)).reshape(shape)
        fz = face(tz_ref[...], m[:-1], m[1:], p[:-1], p[1:])
        zero = jnp.zeros((1, 8, 128), F32)
        total = total + (jnp.concatenate([fz, zero], 0) - jnp.concatenate([zero, fz], 0))
        turned = pltpu.roll(qy_ref[...], (256 - 2 * snap) % 128, 1)
        flat = total.reshape(64, 128) + jnp.where(at_edge, turned, 0.0)
        start = pl.multiple_of(snap * 64, 64)
        flux_ref[pl.ds(start, 64), :] = flat

        def edge(own_ref, other_ref, which):
            s_here = own_ref[64 + snap].astype(F32)
            s_next = other_ref[64 + snap].astype(F32)
            p_here, p_next = own_ref[snap].astype(F32), other_ref[snap].astype(F32)
            return face(txe_ref[which], s_here * s_here, s_next * s_next, p_here, p_next)

        low = pl.ds(start, 8, stride=8)
        high = pl.ds(start + 7, 8, stride=8)
        flux_ref[low, :] = flux_ref[low, :] + edge(low_ref, from_low_ref, 0)
        flux_ref[high, :] = flux_ref[high, :] + edge(high_ref, from_high_ref, 1)
        out_ref[k] = flux_ref[pl.ds(start, 64), :].reshape(shape).astype(BF16)

    @pl.when(step == pl.num_programs(0) - 1)
    def _():
        tile = where_ref[0]
        lane = lax.broadcasted_iota(jnp.int32, (64, 128), 1)

        def pick(i, acc):
            cell = cand_ref[tile, i]
            values = flux_ref[pl.ds(cell // 128, 64, stride=64), :]
            turned = pltpu.roll(values, (i - cell % 128 + 128) % 128, 1)
            return jnp.where(lane == i, turned, acc)

        acc = lax.fori_loop(0, 64, pick, jnp.zeros((64, 128), F32), unroll=4)
        full = jnp.concatenate([acc, jnp.zeros((64, 128), F32)], 0)
        rows_ref[...] = jnp.transpose(full)[:64, :]


def pair_kernel(order_ref, where_ref, mine_ref, other_ref, out_ref, stack_ref):
    tile = where_ref[0]
    core = tile % 2
    node = tile // 2
    stack_ref[pl.ds(pl.multiple_of(core * 64, 64), 64), :] = mine_ref[...]
    stack_ref[pl.ds(pl.multiple_of(64 - core * 64, 64), 64), :] = other_ref[...]
    left, right = [], []
    for r in range(16):
        left.append(stack_ref[pl.ds(order_ref[node, core * 32 + r], 1), :])
        right.append(stack_ref[pl.ds(order_ref[node, core * 32 + 16 + r], 1), :])
    packed = jnp.concatenate(left, 0) + pltpu.roll(jnp.concatenate(right, 0), 64, 1)
    out_ref[...] = jnp.broadcast_to(packed[None], out_ref.shape)


def tree_kernel(where_ref, pick_ref, mine_ref, other_ref, out_ref, half_ref, level_ref):
    core = where_ref[0] % 2
    half_ref[core] = mine_ref[...]
    half_ref[1 - core] = other_ref[...]
    lane = lax.broadcasted_iota(jnp.int32, (16, 128), 1)
    left = lane < 64

    def unpack(chip, carry):
        for half in range(2):
            both = half_ref[half, chip]
            for part in range(2):
                value = both if part == 0 else pltpu.roll(both, 64, 1)
                top = value.astype(BF16).astype(F32)
                rest = value - top
                pieces = jnp.where(left, top, pltpu.roll(rest, 64, 1)).astype(BF16)
                at = half * 32 + part * 16
                out_ref[chip, pl.ds(at, 16), :] = value[:, :64]
                level_ref[chip, pl.ds(at, 16), :] = pieces
        return carry

    lax.fori_loop(0, 64, unpack, 0, unroll=2)
    before, offset, count = 0, 64, 32
    while count >= 1:
        for j in range(count):
            stack = level_ref[pl.ds(before + 2 * j, 2)].reshape(128, 128)
            got = jnp.dot(pick_ref[offset - 64 + j], stack, preferred_element_type=F32)
            level_ref[offset + j] = got.astype(BF16)
            out_ref[offset + j] = (got + pltpu.roll(got, 64, 1))[:, :64]
        before, offset, count = offset, offset + count, count // 2


def whole(shape):
    return pl.BlockSpec(shape, lambda *_: (0,) * len(shape))


SMEM = pl.BlockSpec(memory_space=pltpu.SMEM)
LIMIT = pltpu.CompilerParams(vmem_limit_bytes=48 * 1024 * 1024)


def local(states, class_map, perm_table, candidates, merge_order):
    tile = lax.axis_index("gx") * lax.axis_size("gy") + lax.axis_index("gy")
    where = tile.reshape(1).astype(jnp.int32)
    steps = 64 // CHUNK
    states_spec = pl.BlockSpec((2, CHUNK, 8, 8, 128), lambda i: (0, i, 0, 0, 0))
    edge_shape = jax.ShapeDtypeStruct((129, 8, 128), BF16)
    side_shape = jax.ShapeDtypeStruct((3, 8, 8, 128), BF16)
    low, high, side = pl.pallas_call(
        edge_kernel,
        grid=(steps,),
        in_specs=[states_spec, whole((8, 8, 128))],
        out_specs=[whole((129, 8, 128)), whole((129, 8, 128)), whole((3, 8, 8, 128))],
        out_shape=[edge_shape, edge_shape, side_shape],
        scratch_shapes=[pltpu.VMEM((2 * CHUNK * 64, 128), F32), pltpu.VMEM((2, 64, 128), F32)],
        compiler_params=LIMIT,
    )(states, class_map)

    def shift(value, axis, by):
        count = lax.axis_size(axis)
        return lax.ppermute(value, axis, [(i, (i + by) % count) for i in range(count)])

    from_low = shift(high, "gx", 1)
    from_high = shift(low, "gx", -1)
    side_low = shift(side, "gy", 1)
    side_high = shift(side, "gy", -1)

    flux, rows = pl.pallas_call(
        flux_kernel,
        grid=(steps,),
        in_specs=[SMEM, SMEM, SMEM, states_spec, whole((8, 8, 128))]
        + [whole((129, 8, 128))] * 2 + [whole((3, 8, 8, 128))]
        + [whole((129, 8, 128))] * 2 + [whole((3, 8, 8, 128))] * 2,
        out_specs=[pl.BlockSpec((CHUNK, 8, 8, 128), lambda i: (i, 0, 0, 0)), whole((64, 128))],
        out_shape=[
            jax.ShapeDtypeStruct((64, 8, 8, 128), BF16),
            jax.ShapeDtypeStruct((64, 128), F32),
        ],
        scratch_shapes=[
            pltpu.VMEM((4096, 128), F32),
            pltpu.VMEM((8, 8, 128), F32),
            pltpu.VMEM((8, 8, 128), F32),
            pltpu.VMEM((7, 8, 128), F32),
            pltpu.VMEM((2, 8, 128), F32),
            pltpu.VMEM((64, 128), F32),
        ],
        compiler_params=LIMIT,
    )(
        perm_table, candidates.reshape(128, 64), where, states, class_map, low, high, side,
        from_low, from_high, side_low, side_high,
    )

    swap = [(i, i ^ 1) for i in range(8)]
    other_rows = lax.ppermute(rows, "gy", swap)
    spread = pl.pallas_call(
        pair_kernel,
        in_specs=[SMEM, SMEM, whole((64, 128)), whole((64, 128))],
        out_specs=whole((64, 16, 128)),
        out_shape=jax.ShapeDtypeStruct((64, 16, 128), F32),
        scratch_shapes=[pltpu.VMEM((128, 128), F32)],
        compiler_params=LIMIT,
    )(merge_order, where, rows, other_rows)
    peers = [[i * 8 + j * 2 + c for i in range(16) for j in range(4)] for c in range(2)]
    mine = lax.all_to_all(spread, ("gx", "gy"), 0, 0, axis_index_groups=peers)
    other = lax.ppermute(mine, "gy", swap)

    numbers = lax.broadcasted_iota(jnp.int32, (63, 64, 128), 2)
    picks = (merge_order[64:, :64, None] == numbers).astype(BF16)
    kept = pl.pallas_call(
        tree_kernel,
        in_specs=[SMEM, whole((63, 64, 128)), whole((64, 16, 128)), whole((64, 16, 128))],
        out_specs=whole((127, 64, 64)),
        out_shape=jax.ShapeDtypeStruct((127, 64, 64), F32),
        scratch_shapes=[pltpu.VMEM((2, 64, 16, 128), F32), pltpu.VMEM((127, 64, 128), BF16)],
        compiler_params=LIMIT,
    )(where, picks, mine, other)
    return flux, kept


def solution(mesh):
    in_specs = (P(None, None, None, "gx", "gy"), P(None, "gx", "gy"), P(), P(), P())
    out_specs = (P(None, None, "gx", "gy"), P())
    return jax.shard_map(local, mesh=mesh, in_specs=in_specs, out_specs=out_specs, check_vma=False)
```

```python
import jax
import jax.numpy as jnp
from jax import lax
from jax.experimental import pallas as pl
from jax.experimental.pallas import tpu as pltpu
from jax.sharding import PartitionSpec as P

F32 = jnp.float32
BF16 = jnp.bfloat16
PARTS = 8
PER = 64 // PARTS
CUBE = (8, 8, 128)
FLAT = (64, 128)
HBM = pl.BlockSpec(memory_space=pltpu.HBM)
SMEM = pl.BlockSpec(memory_space=pltpu.SMEM)
LIMIT = pltpu.CompilerParams(vmem_limit_bytes=48 * 1024 * 1024)


def whole(shape):
    return pl.BlockSpec(shape, lambda *_: (0,) * len(shape))


def lane_of(shape):
    return lax.broadcasted_iota(jnp.int32, shape, len(shape) - 1)


def turn(value, by):
    return pltpu.roll(value, by, 1)


def look_up(kind, table_ref):
    value = jnp.zeros(kind.shape, F32)
    for number in range(8):
        value = jnp.where(kind == number, table_ref[number], value)
    return value


def trans(k_here, k_next):
    return k_here * k_next / (k_here + k_next)


def face(t, m_here, m_next, p_here, p_next):
    return t * (m_here + m_next) * (p_next - p_here)


def three_pieces(value):
    high = value.astype(BF16)
    rest = value - high.astype(F32)
    middle = rest.astype(BF16)
    return high, middle, (rest - middle.astype(F32)).astype(BF16)


def part_copy(states_hbm, states_ref, sem, part):
    span = pl.ds(part * PER, PER)
    return pltpu.make_async_copy(states_hbm.at[:, span], states_ref.at[:, span], sem.at[part])


def edge_kernel(
    table_hbm, class_hbm, states_hbm, low_ref, high_ref, side_ref,
    states_ref, class_ref, table_ref, wide_ref, sem, small_sem,
):
    get_table = pltpu.make_async_copy(table_hbm, table_ref, small_sem.at[0])
    get_class = pltpu.make_async_copy(class_hbm, class_ref, small_sem.at[1])
    get_table.start()
    get_class.start()
    for part in range(PARTS):
        part_copy(states_hbm, states_ref, sem, part).start()
    lane = lane_of(FLAT)
    get_table.wait()
    get_class.wait()
    perm = look_up(class_ref[...], table_ref)
    wide_ref[pl.ds(0, 64), :] = perm.reshape(FLAT)
    for ref, at in ((low_ref, 0), (high_ref, 7)):
        for n, piece in enumerate(three_pieces(wide_ref[pl.ds(at, 8, stride=8), :])):
            ref[128 + n] = piece
    first = jnp.broadcast_to(perm[:, :, 0:1], CUBE)
    last = jnp.broadcast_to(perm[:, :, 127:128], CUBE)
    for n, piece in enumerate(three_pieces(jnp.where(lane_of(CUBE) % 2 == 0, first, last))):
        side_ref[2 + n] = piece
    acc = [jnp.zeros(FLAT, F32), jnp.zeros(FLAT, F32)]
    for part in range(PARTS):
        part_copy(states_hbm, states_ref, sem, part).wait()
        for k in range(PER):
            snap = part * PER + k
            for field in range(2):
                value = states_ref[field, snap].astype(F32).reshape(FLAT)
                slot = (1 + field + 2 * snap) * 64
                wide_ref[pl.ds(slot, 64), :] = value
                keep = (lane == 2 * snap) | (lane == (2 * snap + 127) % 128)
                acc[field] = jnp.where(keep, turn(value, 2 * snap), acc[field])
                low_ref[field * 64 + snap] = wide_ref[pl.ds(slot, 8, stride=8), :].astype(BF16)
                high_ref[field * 64 + snap] = wide_ref[pl.ds(slot + 7, 8, stride=8), :].astype(BF16)
    for field in range(2):
        side_ref[field] = acc[field].reshape(CUBE).astype(BF16)


def inner_kernel(
    table_hbm, class_hbm, states_hbm, out_ref,
    states_ref, class_ref, table_ref, tx_ref, ty_ref, tz_ref, sem, small_sem,
):
    get_table = pltpu.make_async_copy(table_hbm, table_ref, small_sem.at[0])
    get_class = pltpu.make_async_copy(class_hbm, class_ref, small_sem.at[1])
    get_table.start()
    get_class.start()
    for part in range(PARTS):
        part_copy(states_hbm, states_ref, sem, part).start()
    get_table.wait()
    get_class.wait()
    perm = look_up(class_ref[...], table_ref)
    row = lax.broadcasted_iota(jnp.int32, CUBE, 1)
    next_y = turn(perm.reshape(FLAT), 127).reshape(CUBE)
    tx_ref[...] = jnp.where(row == 7, 0.0, trans(perm, jnp.roll(perm, -1, 1)))
    ty_ref[...] = jnp.where(lane_of(CUBE) == 127, 0.0, trans(perm, next_y))
    tz_ref[...] = trans(perm[:-1], perm[1:])
    for part in range(PARTS):
        part_copy(states_hbm, states_ref, sem, part).wait()
        for k in range(PER):
            snap = part * PER + k
            p = states_ref[0, snap].astype(F32)
            s = states_ref[1, snap].astype(F32)
            m = s * s
            fx = face(tx_ref[...], m, jnp.roll(m, -1, 1), p, jnp.roll(p, -1, 1))
            total = fx - jnp.roll(fx, 1, 1)
            pf, mf = p.reshape(FLAT), m.reshape(FLAT)
            fy = face(ty_ref[...].reshape(FLAT), mf, turn(mf, 127), pf, turn(pf, 127))
            total = total + (fy - turn(fy, 1)).reshape(CUBE)
            fz = face(tz_ref[...], m[:-1], m[1:], p[:-1], p[1:])
            zero = jnp.zeros((1, 8, 128), F32)
            total = total + (jnp.concatenate([fz, zero], 0) - jnp.concatenate([zero, fz], 0))
            out_ref[pl.ds(snap * 64, 64), :] = total.reshape(FLAT)


def outer_kernel(
    where_ref, cand_hbm, order_hbm, inner_ref, low_ref, high_ref, side_ref,
    from_low_ref, from_high_ref, side_low_ref, side_high_ref,
    out_hbm, mine_ref, send_ref,
    flux_ref, out_ref, txe_ref, qy_ref, cand_ref, order_ref, sem, small_sem,
):
    tile = where_ref[0]
    core = tile % 2
    get_cand = pltpu.make_async_copy(cand_hbm.at[pl.ds(tile, 1)], cand_ref, small_sem.at[0])
    get_order = pltpu.make_async_copy(order_hbm.at[pl.ds(tile // 2, 1)], order_ref, small_sem.at[1])
    get_cand.start()
    get_order.start()
    lane = lane_of(FLAT)

    def perm_of(ref, at):
        high, middle, low = (ref[at + n].astype(F32) for n in range(3))
        return (high + middle) + low

    txe_ref[0] = trans(perm_of(low_ref, 128), perm_of(from_low_ref, 128))
    txe_ref[1] = trans(perm_of(high_ref, 128), perm_of(from_high_ref, 128))

    def beyond(below, above):
        below, above = below.reshape(FLAT), above.reshape(FLAT)
        return jnp.where(lane % 2 == 0, turn(below, 1), turn(above, 127))

    t_side = trans(
        perm_of(side_ref, 2).reshape(FLAT), beyond(perm_of(side_low_ref, 2), perm_of(side_high_ref, 2))
    )

    def side_pair(which):
        here = side_ref[which].astype(F32).reshape(FLAT)
        return here, beyond(side_low_ref[which].astype(F32), side_high_ref[which].astype(F32))

    p_here, p_next = side_pair(0)
    s_here, s_next = side_pair(1)
    qy_ref[...] = face(t_side, s_here * s_here, s_next * s_next, p_here, p_next)
    at_edge = (lane == 0) | (lane == 127)

    def edge(own_ref, other_ref, which, snap):
        s_here, s_next = own_ref[64 + snap].astype(F32), other_ref[64 + snap].astype(F32)
        p_here, p_next = own_ref[snap].astype(F32), other_ref[snap].astype(F32)
        return face(txe_ref[which], s_here * s_here, s_next * s_next, p_here, p_next)

    def put(part):
        span = pl.ds(part * PER, PER)
        return pltpu.make_async_copy(out_ref.at[span], out_hbm.at[span], sem.at[part])

    for part in range(PARTS):
        for k in range(PER):
            snap = part * PER + k
            start = snap * 64
            turned = turn(qy_ref[...], (128 - 2 * snap) % 128)
            flux_ref[pl.ds(start, 64), :] = inner_ref[pl.ds(start, 64), :] + jnp.where(at_edge, turned, 0.0)
            low, high = pl.ds(start, 8, stride=8), pl.ds(start + 7, 8, stride=8)
            flux_ref[low, :] = flux_ref[low, :] + edge(low_ref, from_low_ref, 0, snap)
            flux_ref[high, :] = flux_ref[high, :] + edge(high_ref, from_high_ref, 1, snap)
        for k in range(PER):
            snap = part * PER + k
            out_ref[snap] = flux_ref[pl.ds(snap * 64, 64), :].reshape(CUBE).astype(BF16)
        put(part).start()

    get_cand.wait()
    get_order.wait()

    def pick(i, acc):
        source = order_ref[0, i]
        cell = cand_ref[0, source % 64]
        slot = (i + 32 * core) % 64
        values = flux_ref[pl.ds(cell // 128, 64, stride=64), :]
        turned = turn(values, (slot - cell % 128 + 128) % 128)
        return jnp.where(lane == jnp.where(source // 64 == core, slot, -1), turned, acc)

    acc = lax.fori_loop(0, 64, pick, jnp.zeros(FLAT, F32), unroll=8)
    rows = jnp.transpose(jnp.concatenate([acc, jnp.zeros(FLAT, F32)], 0))
    mine_ref[...] = rows[:32]
    send_ref[...] = rows[32:64]
    for part in range(PARTS):
        put(part).wait()


def tree_kernel(
    where_ref, pick_ref, mine_ref, other_ref, out_hbm, half_ref, level_ref, kept_ref, out_ref, sem
):
    core = where_ref[0] % 2
    half_ref[core] = mine_ref[...]
    half_ref[1 - core] = other_ref[...]
    left = lane_of((32, 128)) < 64

    def keep(node, upper, lower):
        upper, lower = upper + turn(upper, 64), lower + turn(lower, 64)
        kept_ref[pl.ds(node * 32, 32), :] = jnp.where(left, upper, lower)

    for chip in range(64):
        keep(chip, half_ref[0, chip].astype(F32), half_ref[1, chip].astype(F32))
    before, offset, count = 0, 64, 32
    while count >= 1:
        for j in range(count):
            first = before + 2 * j
            if before == 0:
                stack = jnp.concatenate(
                    [half_ref[0, first], half_ref[1, first], half_ref[0, first + 1], half_ref[1, first + 1]], 0
                )
            else:
                stack = level_ref[pl.ds(first - 64, 2)].reshape(128, 128)
            got = jnp.dot(pick_ref[offset - 64 + j], stack, preferred_element_type=F32)
            level_ref[offset - 64 + j] = got.astype(BF16)
            keep(offset + j, got[:32], got[32:])
        before, offset, count = offset, offset + count, count // 2

    def put(at):
        span = pl.ds(at, 4)
        return pltpu.make_async_copy(out_ref.at[span], out_hbm.at[span], sem.at[at // 4])

    for group in range(8):
        for q in range(4 * group, 4 * group + 4):
            turned = jnp.transpose(kept_ref[pl.ds(q, 128, stride=32), :])
            out_ref[q] = turned[:64, :127]
            out_ref[q + 32] = turned[64:, :127]
        put(4 * group).start()
        put(4 * group + 32).start()
    for at in range(0, 64, 4):
        put(at).wait()


def local(states, class_map, perm_table, candidates, merge_order):
    tile = lax.axis_index("gx") * lax.axis_size("gy") + lax.axis_index("gy")
    where = tile.reshape(1).astype(jnp.int32)
    states, class_map, perm_table, candidates, merge_rows = (
        pltpu.with_memory_space_constraint(value, pltpu.HBM)
        for value in (states, class_map, perm_table, candidates.reshape(128, 64), merge_order)
    )
    edge_shape, side_shape = (131, 8, 128), (5, 8, 8, 128)
    states_scratch = [
        pltpu.VMEM((2, 64, 8, 8, 128), BF16), pltpu.VMEM(CUBE, jnp.int32), pltpu.SMEM((8,), F32)
    ]
    sems = [pltpu.SemaphoreType.DMA((PARTS,)), pltpu.SemaphoreType.DMA((2,))]
    low, high, side = pl.pallas_call(
        edge_kernel,
        in_specs=[HBM, HBM, HBM],
        out_specs=[whole(edge_shape), whole(edge_shape), whole(side_shape)],
        out_shape=[
            jax.ShapeDtypeStruct(edge_shape, BF16),
            jax.ShapeDtypeStruct(edge_shape, BF16),
            jax.ShapeDtypeStruct(side_shape, BF16),
        ],
        scratch_shapes=states_scratch + [pltpu.VMEM((129 * 64, 128), F32)] + sems,
        compiler_params=LIMIT,
    )(perm_table, class_map, states)

    def shift(value, axis, by):
        count = lax.axis_size(axis)
        return lax.ppermute(value, axis, [(i, (i + by) % count) for i in range(count)])

    from_low = shift(high, "gx", 1)
    from_high = shift(low, "gx", -1)
    side_low = shift(side, "gy", 1)
    side_high = shift(side, "gy", -1)

    inner = pl.pallas_call(
        inner_kernel,
        in_specs=[HBM, HBM, HBM],
        out_specs=whole((4096, 128)),
        out_shape=jax.ShapeDtypeStruct((4096, 128), F32),
        scratch_shapes=states_scratch
        + [pltpu.VMEM(CUBE, F32), pltpu.VMEM(CUBE, F32), pltpu.VMEM((7, 8, 128), F32)]
        + sems,
        compiler_params=LIMIT,
    )(perm_table, class_map, states)

    flux, mine_rows, send_rows = pl.pallas_call(
        outer_kernel,
        in_specs=[SMEM, HBM, HBM, whole((4096, 128))]
        + [whole(edge_shape)] * 2 + [whole(side_shape)] + [whole(edge_shape)] * 2 + [whole(side_shape)] * 2,
        out_specs=[HBM, whole((32, 128)), whole((32, 128))],
        out_shape=[
            jax.ShapeDtypeStruct((64, 8, 8, 128), BF16),
            jax.ShapeDtypeStruct((32, 128), F32),
            jax.ShapeDtypeStruct((32, 128), F32),
        ],
        scratch_shapes=[
            pltpu.VMEM((4096, 128), F32),
            pltpu.VMEM((64, 8, 8, 128), BF16),
            pltpu.VMEM((2, 8, 128), F32),
            pltpu.VMEM(FLAT, F32),
            pltpu.SMEM((1, 64), jnp.int32),
            pltpu.SMEM((1, 128), jnp.int32),
        ]
        + sems,
        compiler_params=LIMIT,
    )(
        where, candidates, merge_rows, inner, low, high, side,
        from_low, from_high, side_low, side_high,
    )

    swap = [(i, i ^ 1) for i in range(8)]
    got_rows = lax.ppermute(send_rows, "gy", swap)
    merged = mine_rows[:, :64] + got_rows[:, :64]
    top = merged.astype(BF16)
    rest = (merged - lax.reduce_precision(merged, 8, 7)).astype(BF16)
    spread = jnp.broadcast_to(jnp.concatenate([top, rest], 1)[None], (64, 32, 128))
    peers = [[i * 8 + j * 2 + c for i in range(16) for j in range(4)] for c in range(2)]
    mine = lax.all_to_all(spread, ("gx", "gy"), 0, 0, axis_index_groups=peers)
    other = lax.ppermute(mine, "gy", swap)

    numbers = lax.broadcasted_iota(jnp.int32, (63, 64, 128), 2)
    picks = (merge_order[64:, :64, None] == numbers).astype(BF16)
    kept = pl.pallas_call(
        tree_kernel,
        in_specs=[SMEM, whole((63, 64, 128)), whole((64, 32, 128)), whole((64, 32, 128))],
        out_specs=HBM,
        out_shape=jax.ShapeDtypeStruct((64, 64, 127), F32),
        scratch_shapes=[
            pltpu.VMEM((2, 64, 32, 128), BF16),
            pltpu.VMEM((63, 64, 128), BF16),
            pltpu.VMEM((128 * 32, 128), F32),
            pltpu.VMEM((64, 64, 127), F32),
            pltpu.SemaphoreType.DMA((16,)),
        ],
        compiler_params=LIMIT,
    )(where, picks, mine, other)
    return flux, jnp.transpose(kept, (2, 0, 1))


def solution(mesh):
    in_specs = (P(None, None, None, "gx", "gy"), P(None, "gx", "gy"), P(), P(), P())
    out_specs = (P(None, None, "gx", "gy"), P())
    return jax.shard_map(local, mesh=mesh, in_specs=in_specs, out_specs=out_specs, check_vma=False)
```

```python
import jax
import jax.numpy as jnp
from jax import lax
from jax.experimental import pallas as pl
from jax.experimental.pallas import tpu as pltpu
from jax.sharding import PartitionSpec as P

F32 = jnp.float32
BF16 = jnp.bfloat16
PITCH = 72
CUBE = (8, 8, 128)
FLAT = (64, 128)
HBM = pl.BlockSpec(memory_space=pltpu.HBM)
SMEM = pl.BlockSpec(memory_space=pltpu.SMEM)
LIMIT = pltpu.CompilerParams(vmem_limit_bytes=48 * 1024 * 1024)


def whole(shape):
    return pl.BlockSpec(shape, lambda *_: (0,) * len(shape))


def lane_of(shape):
    return lax.broadcasted_iota(jnp.int32, shape, len(shape) - 1)


def turn(value, by):
    return pltpu.roll(value, by, 1)


def look_up(kind, table_ref):
    value = jnp.zeros(kind.shape, F32)
    for number in range(8):
        value = jnp.where(kind == number, table_ref[number], value)
    return value


def trans(k_here, k_next):
    return k_here * k_next / (k_here + k_next)


def face(t, m_here, m_next, p_here, p_next):
    return t * (m_here + m_next) * (p_next - p_here)


def three_pieces(value):
    high = value.astype(BF16)
    rest = value - high.astype(F32)
    middle = rest.astype(BF16)
    return high, middle, (rest - middle.astype(F32)).astype(BF16)


def edge_x_kernel(
    table_hbm, class_hbm, states_hbm, low_ref, high_ref, states_ref, class_ref, table_ref, wide_ref, sem
):
    copies = [
        pltpu.make_async_copy(table_hbm, table_ref, sem.at[0]),
        pltpu.make_async_copy(class_hbm, class_ref, sem.at[1]),
    ]
    for n, rows in enumerate((pl.ds(0, 2), pl.ds(6, 2))):
        copies.append(
            pltpu.make_async_copy(states_hbm.at[:, :, :, rows], states_ref.at[:, :, :, rows], sem.at[2 + n])
        )
    for copy in copies:
        copy.start()
    copies[0].wait()
    copies[1].wait()
    wide_ref[pl.ds(0, 64), :] = look_up(class_ref[...], table_ref).reshape(FLAT)
    for ref, at in ((low_ref, 0), (high_ref, 7)):
        for n, piece in enumerate(three_pieces(wide_ref[pl.ds(at, 8, stride=8), :])):
            ref[128 + n] = piece
    copies[2].wait()
    copies[3].wait()
    for snap in range(64):
        for field in range(2):
            slot = (1 + field + 2 * snap) * 64
            wide_ref[pl.ds(slot, 64), :] = states_ref[field, snap].astype(F32).reshape(FLAT)
            low_ref[field * 64 + snap] = wide_ref[pl.ds(slot, 8, stride=8), :].astype(BF16)
            high_ref[field * 64 + snap] = wide_ref[pl.ds(slot + 7, 8, stride=8), :].astype(BF16)


def edge_y_kernel(table_hbm, class_hbm, states_hbm, side_ref, perm_ref, states_ref, class_ref, table_ref, sem):
    copies = [
        pltpu.make_async_copy(table_hbm, table_ref, sem.at[0]),
        pltpu.make_async_copy(class_hbm, class_ref, sem.at[1]),
    ]
    for n in range(2):
        half = pl.ds(32 * n, 32)
        copies.append(pltpu.make_async_copy(states_hbm.at[:, half], states_ref.at[:, half], sem.at[2 + n]))
    for copy in copies:
        copy.start()
    copies[0].wait()
    copies[1].wait()
    perm = look_up(class_ref[...], table_ref)
    perm_ref[...] = perm
    first = jnp.broadcast_to(perm[:, :, 0:1], CUBE)
    last = jnp.broadcast_to(perm[:, :, 127:128], CUBE)
    for n, piece in enumerate(three_pieces(jnp.where(lane_of(CUBE) % 2 == 0, first, last))):
        side_ref[2 + n] = piece
    lane = lane_of(FLAT)
    acc = [jnp.zeros(FLAT, F32), jnp.zeros(FLAT, F32)]
    for snap in range(64):
        if snap % 32 == 0:
            copies[2 + snap // 32].wait()
        keep = (lane == 2 * snap) | (lane == (2 * snap + 127) % 128)
        for field in range(2):
            value = states_ref[field, snap].astype(F32).reshape(FLAT)
            acc[field] = jnp.where(keep, turn(value, 2 * snap), acc[field])
    for field in range(2):
        side_ref[field] = acc[field].reshape(CUBE).astype(BF16)


def inner_kernel(perm_ref, states_ref, out_ref, tx_ref, ty_ref, tz_ref):
    perm = perm_ref[...]
    row = lax.broadcasted_iota(jnp.int32, CUBE, 1)
    next_y = turn(perm.reshape(FLAT), 127).reshape(CUBE)
    tx_ref[...] = jnp.where(row == 7, 0.0, trans(perm, jnp.roll(perm, -1, 1)))
    ty_ref[...] = jnp.where(lane_of(CUBE) == 127, 0.0, trans(perm, next_y))
    tz_ref[...] = trans(perm[:-1], perm[1:])

    def group(number, carry):
        for k in range(16):
            snap = number * 16 + k
            p = states_ref[0, snap].astype(F32)
            s = states_ref[1, snap].astype(F32)
            m = s * s
            fx = face(tx_ref[...], m, jnp.roll(m, -1, 1), p, jnp.roll(p, -1, 1))
            total = fx - jnp.roll(fx, 1, 1)
            pf, mf = p.reshape(FLAT), m.reshape(FLAT)
            fy = face(ty_ref[...].reshape(FLAT), mf, turn(mf, 127), pf, turn(pf, 127))
            total = total + (fy - turn(fy, 1)).reshape(CUBE)
            fz = face(tz_ref[...], m[:-1], m[1:], p[:-1], p[1:])
            zero = jnp.zeros((1, 8, 128), F32)
            total = total + (jnp.concatenate([fz, zero], 0) - jnp.concatenate([zero, fz], 0))
            out_ref[pl.ds(pl.multiple_of(snap * 64, 64), 64), :] = total.reshape(FLAT)
        return carry

    lax.fori_loop(0, 4, group, 0)


def outer_kernel(
    where_ref, cand_hbm, order_hbm, inner_ref, low_ref, high_ref, side_ref,
    from_low_ref, from_high_ref, side_low_ref, side_high_ref,
    out_hbm, mine_ref, send_ref,
    flux_ref, out_ref, txe_ref, qy_ref, cand_ref, order_ref, sem, small_sem,
):
    tile = where_ref[0]
    core = tile % 2
    get_cand = pltpu.make_async_copy(cand_hbm.at[pl.ds(tile, 1)], cand_ref, small_sem.at[0])
    get_order = pltpu.make_async_copy(order_hbm.at[pl.ds(tile // 2, 1)], order_ref, small_sem.at[1])
    get_cand.start()
    get_order.start()
    lane = lane_of(FLAT)

    def perm_of(ref, at):
        high, middle, low = (ref[at + n].astype(F32) for n in range(3))
        return (high + middle) + low

    txe_ref[0] = trans(perm_of(low_ref, 128), perm_of(from_low_ref, 128))
    txe_ref[1] = trans(perm_of(high_ref, 128), perm_of(from_high_ref, 128))

    def beyond(below, above):
        below, above = below.reshape(FLAT), above.reshape(FLAT)
        return jnp.where(lane % 2 == 0, turn(below, 1), turn(above, 127))

    t_side = trans(
        perm_of(side_ref, 2).reshape(FLAT), beyond(perm_of(side_low_ref, 2), perm_of(side_high_ref, 2))
    )

    def side_pair(which):
        here = side_ref[which].astype(F32).reshape(FLAT)
        return here, beyond(side_low_ref[which].astype(F32), side_high_ref[which].astype(F32))

    p_here, p_next = side_pair(0)
    s_here, s_next = side_pair(1)
    qy_ref[...] = face(t_side, s_here * s_here, s_next * s_next, p_here, p_next)
    at_edge = (lane == 0) | (lane == 127)

    def edge(own_ref, other_ref, which, snap):
        s_here, s_next = own_ref[64 + snap].astype(F32), other_ref[64 + snap].astype(F32)
        p_here, p_next = own_ref[snap].astype(F32), other_ref[snap].astype(F32)
        return face(txe_ref[which], s_here * s_here, s_next * s_next, p_here, p_next)

    def put(part):
        span = pl.ds(part * 32, 32)
        return pltpu.make_async_copy(out_ref.at[span], out_hbm.at[span], sem.at[part])

    def group(number, carry):
        for k in range(16):
            snap = number * 16 + k
            start = pl.multiple_of(snap * PITCH, 8)
            turned = turn(qy_ref[...], (128 - 2 * snap) % 128)
            within = inner_ref[pl.ds(pl.multiple_of(snap * 64, 64), 64), :]
            flux_ref[pl.ds(start, 64), :] = within + jnp.where(at_edge, turned, 0.0)
            low, high = pl.ds(start, 8, stride=8), pl.ds(start + 7, 8, stride=8)
            flux_ref[low, :] = flux_ref[low, :] + edge(low_ref, from_low_ref, 0, snap)
            flux_ref[high, :] = flux_ref[high, :] + edge(high_ref, from_high_ref, 1, snap)
        for k in range(16):
            snap = number * 16 + k
            start = pl.multiple_of(snap * PITCH, 8)
            out_ref[snap] = flux_ref[pl.ds(start, 64), :].reshape(CUBE).astype(BF16)
        return carry

    for part in range(2):
        lax.fori_loop(2 * part, 2 * part + 2, group, 0)
        put(part).start()

    get_cand.wait()
    get_order.wait()

    def pick(i, acc):
        source = order_ref[0, i]
        cell = cand_ref[0, source % 64]
        slot = (i + 32 * core) % 64
        values = flux_ref[pl.ds(cell // 128, 64, stride=PITCH), :]
        turned = turn(values, (slot - cell % 128 + 128) % 128)
        return jnp.where(lane == jnp.where(source // 64 == core, slot, -1), turned, acc)

    acc = lax.fori_loop(0, 64, pick, jnp.zeros(FLAT, F32), unroll=8)
    rows = jnp.transpose(jnp.concatenate([acc, jnp.zeros(FLAT, F32)], 0))
    mine_ref[...] = rows[:32]
    send_ref[...] = rows[32:64]
    for part in range(2):
        put(part).wait()


def tree_kernel(
    where_ref, pick_ref, mine_ref, other_ref, out_hbm, half_ref, level_ref, kept_ref, out_ref, sem
):
    core = where_ref[0] % 2
    half_ref[core] = mine_ref[...]
    half_ref[1 - core] = other_ref[...]
    left = lane_of((32, 128)) < 64

    def keep(node, upper, lower):
        upper, lower = upper + turn(upper, 64), lower + turn(lower, 64)
        kept_ref[pl.ds(node * 32, 32), :] = jnp.where(left, upper, lower)

    for chip in range(64):
        keep(chip, half_ref[0, chip].astype(F32), half_ref[1, chip].astype(F32))
    before, offset, count = 0, 64, 32
    while count >= 1:
        for j in range(count):
            first = before + 2 * j
            if before == 0:
                stack = jnp.concatenate(
                    [half_ref[0, first], half_ref[1, first], half_ref[0, first + 1], half_ref[1, first + 1]], 0
                )
            else:
                stack = level_ref[pl.ds(first - 64, 2)].reshape(128, 128)
            got = jnp.dot(pick_ref[offset - 64 + j], stack, preferred_element_type=F32)
            level_ref[offset - 64 + j] = got.astype(BF16)
            keep(offset + j, got[:32], got[32:])
        before, offset, count = offset, offset + count, count // 2

    def put(at):
        span = pl.ds(at, 4)
        return pltpu.make_async_copy(out_ref.at[span], out_hbm.at[span], sem.at[at // 4])

    for group in range(8):
        for q in range(4 * group, 4 * group + 4):
            turned = jnp.transpose(kept_ref[pl.ds(q, 128, stride=32), :])
            out_ref[q] = turned[:64, :127]
            out_ref[q + 32] = turned[64:, :127]
        put(4 * group).start()
        put(4 * group + 32).start()
    for at in range(0, 64, 4):
        put(at).wait()


def local(states, class_map, perm_table, candidates, merge_order):
    tile = lax.axis_index("gx") * lax.axis_size("gy") + lax.axis_index("gy")
    where = tile.reshape(1).astype(jnp.int32)
    states, class_map, perm_table, candidates, merge_rows = (
        pltpu.with_memory_space_constraint(value, pltpu.HBM)
        for value in (states, class_map, perm_table, candidates.reshape(128, 64), merge_order)
    )
    edge_shape, side_shape, states_shape = (131, 8, 128), (5, 8, 8, 128), (2, 64, 8, 8, 128)
    read_scratch = [pltpu.VMEM(CUBE, jnp.int32), pltpu.SMEM((8,), F32)]
    low, high = pl.pallas_call(
        edge_x_kernel,
        in_specs=[HBM, HBM, HBM],
        out_specs=[whole(edge_shape), whole(edge_shape)],
        out_shape=[jax.ShapeDtypeStruct(edge_shape, BF16), jax.ShapeDtypeStruct(edge_shape, BF16)],
        scratch_shapes=[pltpu.VMEM(states_shape, BF16)]
        + read_scratch
        + [pltpu.VMEM((129 * 64, 128), F32), pltpu.SemaphoreType.DMA((4,))],
        compiler_params=LIMIT,
    )(perm_table, class_map, states)

    def shift(value, axis, by):
        count = lax.axis_size(axis)
        return lax.ppermute(value, axis, [(i, (i + by) % count) for i in range(count)])

    from_low = shift(high, "gx", 1)
    from_high = shift(low, "gx", -1)

    side, perm, near_states = pl.pallas_call(
        edge_y_kernel,
        in_specs=[HBM, HBM, HBM],
        out_specs=[whole(side_shape), whole(CUBE), whole(states_shape)],
        out_shape=[
            jax.ShapeDtypeStruct(side_shape, BF16),
            jax.ShapeDtypeStruct(CUBE, F32),
            jax.ShapeDtypeStruct(states_shape, BF16),
        ],
        scratch_shapes=read_scratch + [pltpu.SemaphoreType.DMA((4,))],
        compiler_params=LIMIT,
    )(perm_table, class_map, states)
    side_low = shift(side, "gy", 1)
    side_high = shift(side, "gy", -1)

    inner = pl.pallas_call(
        inner_kernel,
        in_specs=[whole(CUBE), whole(states_shape)],
        out_specs=whole((4096, 128)),
        out_shape=jax.ShapeDtypeStruct((4096, 128), F32),
        scratch_shapes=[pltpu.VMEM(CUBE, F32), pltpu.VMEM(CUBE, F32), pltpu.VMEM((7, 8, 128), F32)],
        compiler_params=LIMIT,
    )(perm, near_states)

    flux, mine_rows, send_rows = pl.pallas_call(
        outer_kernel,
        in_specs=[SMEM, HBM, HBM, whole((4096, 128))]
        + [whole(edge_shape)] * 2 + [whole(side_shape)] + [whole(edge_shape)] * 2 + [whole(side_shape)] * 2,
        out_specs=[HBM, whole((32, 128)), whole((32, 128))],
        out_shape=[
            jax.ShapeDtypeStruct((64, 8, 8, 128), BF16),
            jax.ShapeDtypeStruct((32, 128), F32),
            jax.ShapeDtypeStruct((32, 128), F32),
        ],
        scratch_shapes=[
            pltpu.VMEM((64 * PITCH, 128), F32),
            pltpu.VMEM((64, 8, 8, 128), BF16),
            pltpu.VMEM((2, 8, 128), F32),
            pltpu.VMEM(FLAT, F32),
            pltpu.SMEM((1, 64), jnp.int32),
            pltpu.SMEM((1, 128), jnp.int32),
            pltpu.SemaphoreType.DMA((2,)),
            pltpu.SemaphoreType.DMA((2,)),
        ],
        compiler_params=LIMIT,
    )(
        where, candidates, merge_rows, inner, low, high, side,
        from_low, from_high, side_low, side_high,
    )

    swap = [(i, i ^ 1) for i in range(8)]
    got_rows = lax.ppermute(send_rows, "gy", swap)
    merged = mine_rows[:, :64] + got_rows[:, :64]
    top = merged.astype(BF16)
    rest = (merged - lax.reduce_precision(merged, 8, 7)).astype(BF16)
    spread = jnp.broadcast_to(jnp.concatenate([top, rest], 1)[None], (64, 32, 128))
    peers = [[i * 8 + j * 2 + c for i in range(16) for j in range(4)] for c in range(2)]
    mine = lax.all_to_all(spread, ("gx", "gy"), 0, 0, axis_index_groups=peers)
    other = lax.ppermute(mine, "gy", swap)

    numbers = lax.broadcasted_iota(jnp.int32, (63, 64, 128), 2)
    picks = (merge_order[64:, :64, None] == numbers).astype(BF16)
    kept = pl.pallas_call(
        tree_kernel,
        in_specs=[SMEM, whole((63, 64, 128)), whole((64, 32, 128)), whole((64, 32, 128))],
        out_specs=HBM,
        out_shape=jax.ShapeDtypeStruct((64, 64, 127), F32),
        scratch_shapes=[
            pltpu.VMEM((2, 64, 32, 128), BF16),
            pltpu.VMEM((63, 64, 128), BF16),
            pltpu.VMEM((128 * 32, 128), F32),
            pltpu.VMEM((64, 64, 127), F32),
            pltpu.SemaphoreType.DMA((16,)),
        ],
        compiler_params=LIMIT,
    )(where, picks, mine, other)
    return flux, jnp.transpose(kept, (2, 0, 1))


def solution(mesh):
    in_specs = (P(None, None, None, "gx", "gy"), P(None, "gx", "gy"), P(), P(), P())
    out_specs = (P(None, None, "gx", "gy"), P())
    return jax.shard_map(local, mesh=mesh, in_specs=in_specs, out_specs=out_specs, check_vma=False)
```

```python
import jax
import jax.numpy as jnp
from jax import lax
from jax.experimental import pallas as pl
from jax.experimental.pallas import tpu as pltpu
from jax.sharding import PartitionSpec as P

F32 = jnp.float32
BF16 = jnp.bfloat16
KEPT = 40
CUBE = (8, 8, 128)
FLAT = (64, 128)
HBM = pl.BlockSpec(memory_space=pltpu.HBM)
SMEM = pl.BlockSpec(memory_space=pltpu.SMEM)
LIMIT = pltpu.CompilerParams(vmem_limit_bytes=48 * 1024 * 1024)


def whole(shape):
    return pl.BlockSpec(shape, lambda *_: (0,) * len(shape))


def lane_of(shape):
    return lax.broadcasted_iota(jnp.int32, shape, len(shape) - 1)


def turn(value, by):
    return pltpu.roll(value, by, 1)


def look_up(kind, table_ref):
    value = jnp.zeros(kind.shape, F32)
    for number in range(8):
        value = jnp.where(kind == number, table_ref[number], value)
    return value


def trans(k_here, k_next):
    return k_here * k_next / (k_here + k_next)


def face(t, m_here, m_next, p_here, p_next):
    return t * (m_here + m_next) * (p_next - p_here)


def three_pieces(value):
    high = value.astype(BF16)
    rest = value - high.astype(F32)
    middle = rest.astype(BF16)
    return high, middle, (rest - middle.astype(F32)).astype(BF16)


def edge_x_kernel(
    table_hbm, class_hbm, states_hbm, low_ref, high_ref, states_ref, class_ref, table_ref, wide_ref, sem
):
    copies = [
        pltpu.make_async_copy(table_hbm, table_ref, sem.at[0]),
        pltpu.make_async_copy(class_hbm, class_ref, sem.at[1]),
    ]
    for n, rows in enumerate((pl.ds(0, 2), pl.ds(6, 2))):
        copies.append(
            pltpu.make_async_copy(states_hbm.at[:, :, :, rows], states_ref.at[:, :, :, rows], sem.at[2 + n])
        )
    for copy in copies:
        copy.start()
    copies[0].wait()
    copies[1].wait()
    wide_ref[pl.ds(0, 64), :] = look_up(class_ref[...], table_ref).reshape(FLAT)
    for ref, at in ((low_ref, 0), (high_ref, 7)):
        for n, piece in enumerate(three_pieces(wide_ref[pl.ds(at, 8, stride=8), :])):
            ref[128 + n] = piece
    copies[2].wait()
    copies[3].wait()
    for snap in range(64):
        for field in range(2):
            slot = (1 + field + 2 * snap) * 64
            wide_ref[pl.ds(slot, 64), :] = states_ref[field, snap].astype(F32).reshape(FLAT)
            low_ref[field * 64 + snap] = wide_ref[pl.ds(slot, 8, stride=8), :].astype(BF16)
            high_ref[field * 64 + snap] = wide_ref[pl.ds(slot + 7, 8, stride=8), :].astype(BF16)


def two_times(weights):
    return jnp.concatenate([weights, weights], 0)


def two_pieces(value):
    high = value.astype(BF16)
    return jnp.concatenate([high, (value - high.astype(F32)).astype(BF16)], 1)


def matmul(left, right):
    return jnp.dot(left, right, preferred_element_type=F32)


def sub_of(shape):
    return lax.broadcasted_iota(jnp.int32, shape, 0)


def edge_y_kernel(
    where_ref, table_hbm, class_hbm, cand_hbm, order_hbm, states_hbm,
    side_ref, perm_ref, states_ref, cells_ref, hits_ref, class_ref, cand_ref, order_ref, table_ref, sem,
):
    tile = where_ref[0]
    core = tile % 2
    copies = [
        pltpu.make_async_copy(table_hbm, table_ref, sem.at[0]),
        pltpu.make_async_copy(class_hbm, class_ref, sem.at[1]),
        pltpu.make_async_copy(cand_hbm.at[pl.ds(tile, 1)], cand_ref, sem.at[2]),
        pltpu.make_async_copy(order_hbm.at[pl.ds(tile // 2, 1)], order_ref, sem.at[3]),
    ]
    for n in range(2):
        half = pl.ds(32 * n, 32)
        copies.append(pltpu.make_async_copy(states_hbm.at[:, half], states_ref.at[:, half], sem.at[4 + n]))
    for copy in copies:
        copy.start()
    for copy in copies[:4]:
        copy.wait()
    lane = lane_of(FLAT)
    order = jnp.broadcast_to(order_ref[...], FLAT)
    swapped = jnp.where(lane < 32, turn(order, 96), turn(order, 32))
    order = jnp.where(core == 1, swapped, order)
    match = (order == core * 64 + sub_of(FLAT)) & (lane < 64)
    column = jnp.transpose(jnp.broadcast_to(cand_ref[...].astype(F32), (64, 64)))[:, :1]
    cell = jnp.sum(jnp.where(match, jnp.broadcast_to(column, FLAT) + 1.0, 0.0), 0, keepdims=True)
    cell = cell.astype(jnp.int32) - 1
    at_y = jnp.where(cell < 0, -1, cell % 128)
    at_zx = jnp.where(cell < 0, -1, cell // 128)
    cells_ref[...] = two_times(jnp.where(sub_of((128, 128)) == at_y, 1.0, 0.0).astype(BF16))
    hits_ref[...] = jnp.where(sub_of(FLAT) == at_zx, 1.0, 0.0).reshape(CUBE)

    perm = look_up(class_ref[...], table_ref)
    perm_ref[...] = perm
    first = jnp.broadcast_to(perm[:, :, 0:1], CUBE)
    last = jnp.broadcast_to(perm[:, :, 127:128], CUBE)
    for n, piece in enumerate(three_pieces(jnp.where(lane_of(CUBE) % 2 == 0, first, last))):
        side_ref[2 + n] = piece
    square = (128, 128)
    spread = jnp.where(sub_of(square) == jnp.where(lane_of(square) % 2 == 0, 0, 127), 1.0, 0.0).astype(BF16)
    acc = [jnp.zeros(FLAT, F32), jnp.zeros(FLAT, F32)]
    for snap in range(64):
        if snap % 32 == 0:
            copies[4 + snap // 32].wait()
        keep = (lane == 2 * snap) | (lane == (2 * snap + 127) % 128)
        for field in range(2):
            value = matmul(states_ref[field, snap].reshape(FLAT), spread)
            acc[field] = jnp.where(keep, value, acc[field])
    for field in range(2):
        side_ref[field] = acc[field].reshape(CUBE).astype(BF16)


def inner_kernel(perm_ref, states_ref, out_ref, tx_ref, ty_ref, tz_ref, shift_ref, differ_ref):
    perm = perm_ref[...]
    row = lax.broadcasted_iota(jnp.int32, CUBE, 1)
    next_y = turn(perm.reshape(FLAT), 127).reshape(CUBE)
    tx_ref[...] = jnp.where(row == 7, 0.0, trans(perm, jnp.roll(perm, -1, 1)))
    ty_ref[...] = jnp.where(lane_of(CUBE) == 127, 0.0, trans(perm, next_y)).reshape(FLAT)
    tz_ref[...] = trans(perm[:-1], perm[1:])
    square = (128, 128)
    ahead = sub_of(square) - lane_of(square)
    shift_ref[...] = jnp.where(ahead == 1, 1.0, 0.0).astype(BF16)
    differ_ref[...] = two_times((jnp.where(ahead == 0, 1.0, 0.0) - jnp.where(ahead == -1, 1.0, 0.0)).astype(BF16))

    def group(number, carry):
        for k in range(8):
            snap = number * 8 + k
            p = states_ref[0, snap].astype(F32)
            s = states_ref[1, snap].astype(F32)
            m = s * s
            fx = face(tx_ref[...], m, jnp.roll(m, -1, 1), p, jnp.roll(p, -1, 1))
            total = fx - jnp.roll(fx, 1, 1)
            p_next = matmul(states_ref[0, snap].reshape(FLAT), shift_ref[...])
            s_next = matmul(states_ref[1, snap].reshape(FLAT), shift_ref[...])
            fy = face(ty_ref[...], m.reshape(FLAT), s_next * s_next, p.reshape(FLAT), p_next)
            total = total + matmul(two_pieces(fy), differ_ref[...]).reshape(CUBE)
            fz = face(tz_ref[...], m[:-1], m[1:], p[:-1], p[1:])
            zero = jnp.zeros((1, 8, 128), F32)
            total = total + (jnp.concatenate([fz, zero], 0) - jnp.concatenate([zero, fz], 0))
            out_ref[pl.ds(pl.multiple_of(snap * 64, 64), 64), :] = total.reshape(FLAT)
        return carry

    lax.fori_loop(0, 8, group, 0)


def outer_kernel(
    inner_ref, cells_ref, hits_ref, low_ref, high_ref, side_ref,
    from_low_ref, from_high_ref, side_low_ref, side_high_ref,
    out_hbm, mine_ref, send_ref,
    flux_ref, out_ref, txe_ref, qy_ref, ends_ref, picked_ref, sem,
):
    lane = lane_of(FLAT)

    def perm_of(ref, at):
        high, middle, low = (ref[at + n].astype(F32) for n in range(3))
        return (high + middle) + low

    txe_ref[0] = trans(perm_of(low_ref, 128), perm_of(from_low_ref, 128))
    txe_ref[1] = trans(perm_of(high_ref, 128), perm_of(from_high_ref, 128))

    def beyond(below, above):
        below, above = below.reshape(FLAT), above.reshape(FLAT)
        return jnp.where(lane % 2 == 0, turn(below, 1), turn(above, 127))

    t_side = trans(
        perm_of(side_ref, 2).reshape(FLAT), beyond(perm_of(side_low_ref, 2), perm_of(side_high_ref, 2))
    )

    def side_pair(which):
        here = side_ref[which].astype(F32).reshape(FLAT)
        return here, beyond(side_low_ref[which].astype(F32), side_high_ref[which].astype(F32))

    p_here, p_next = side_pair(0)
    s_here, s_next = side_pair(1)
    qy_ref[...] = two_pieces(face(t_side, s_here * s_here, s_next * s_next, p_here, p_next))
    square = (128, 128)
    ends = lane_of(square) == jnp.where(sub_of(square) % 2 == 0, 0, 127)
    ends_ref[...] = two_times(jnp.where(ends, 1.0, 0.0).astype(BF16))
    lane_row = lane_of((1, 128))

    def edge(own_ref, other_ref, which, snap):
        s_here, s_next = own_ref[64 + snap].astype(F32), other_ref[64 + snap].astype(F32)
        p_here, p_next = own_ref[snap].astype(F32), other_ref[snap].astype(F32)
        return face(txe_ref[which], s_here * s_here, s_next * s_next, p_here, p_next)

    def put(part):
        span = pl.ds(part * 32, 32)
        return pltpu.make_async_copy(out_ref.at[span], out_hbm.at[span], sem.at[part])

    def group(number, carry):
        for k in range(8):
            snap = number * 8 + k
            start = pl.multiple_of(snap * 64, 64)
            here = (lane_row == 2 * snap) | (lane_row == (2 * snap + 127) % 128)
            here = jnp.where(here, 1.0, 0.0).astype(BF16)
            sides = matmul(qy_ref[...] * jnp.concatenate([here, here], 1), ends_ref[...])
            flux_ref[pl.ds(start, 64), :] = inner_ref[pl.ds(start, 64), :] + sides
            low, high = pl.ds(start, 8, stride=8), pl.ds(start + 7, 8, stride=8)
            flux_ref[low, :] = flux_ref[low, :] + edge(low_ref, from_low_ref, 0, snap)
            flux_ref[high, :] = flux_ref[high, :] + edge(high_ref, from_high_ref, 1, snap)
        for k in range(8):
            snap = number * 8 + k
            flux = flux_ref[pl.ds(pl.multiple_of(snap * 64, 64), 64), :]
            out_ref[snap] = flux.reshape(CUBE).astype(BF16)
            rows = matmul(two_pieces(flux), cells_ref[...]).reshape(CUBE) * hits_ref[...]
            picked_ref[pl.ds(pl.multiple_of(snap * 8, 8), 8), :] = jnp.sum(rows, 0)
        return carry

    for part in range(2):
        lax.fori_loop(4 * part, 4 * part + 4, group, 0)
        put(part).start()

    total = picked_ref[pl.ds(0, 64, stride=8), :]
    for x in range(1, 8):
        total = total + picked_ref[pl.ds(x, 64, stride=8), :]
    rows = jnp.transpose(jnp.concatenate([total, jnp.zeros(FLAT, F32)], 0))
    mine_ref[...] = rows[:32]
    send_ref[...] = rows[32:64]
    for part in range(2):
        put(part).wait()


def tree_kernel(where_ref, pick_ref, mine_ref, other_ref, out_hbm, level_ref, kept_ref, out_ref, weights_ref, sem):
    tall = (256, 128)
    same = (sub_of(tall) % 64 == lane_of(tall) % 64) & (sub_of(tall) // 128 == lane_of(tall) // 64)
    weights_ref[...] = jnp.where(same, 1.0, 0.0).astype(BF16)

    def keep(node, upper, lower):
        both = matmul(jnp.concatenate([upper, lower], 1), weights_ref[...])
        kept_ref[pl.ds(node * KEPT, 32), :] = both

    def select(node, stack):
        rows = matmul(pick_ref[node - 64], stack).astype(BF16)
        level_ref[node - 64] = rows
        keep(node, rows[:32], rows[32:])

    def first_levels(low_ref, high_ref):
        for chip in range(64):
            keep(chip, low_ref[chip], high_ref[chip])
        for j in range(32):
            pair = [low_ref[2 * j], high_ref[2 * j], low_ref[2 * j + 1], high_ref[2 * j + 1]]
            select(64 + j, jnp.concatenate(pair, 0))

    @pl.when(where_ref[0] % 2 == 0)
    def _():
        first_levels(mine_ref, other_ref)

    @pl.when(where_ref[0] % 2 == 1)
    def _():
        first_levels(other_ref, mine_ref)

    before, offset, count = 64, 96, 16
    while count >= 1:
        for j in range(count):
            select(offset + j, level_ref[pl.ds(before + 2 * j - 64, 2)].reshape(128, 128))
        before, offset, count = offset, offset + count, count // 2

    def put(at):
        span = pl.ds(at, 8)
        return pltpu.make_async_copy(out_ref.at[span], out_hbm.at[span], sem.at[at // 8])

    for group in range(4):
        for q in range(8 * group, 8 * group + 8):
            turned = jnp.transpose(kept_ref[pl.ds(q, 128, stride=KEPT), :])
            out_ref[q] = turned[:64, :127]
            out_ref[q + 32] = turned[64:, :127]
        put(8 * group).start()
        put(8 * group + 32).start()
    for at in range(0, 64, 8):
        put(at).wait()


def local(states, class_map, perm_table, candidates, merge_order):
    tile = lax.axis_index("gx") * lax.axis_size("gy") + lax.axis_index("gy")
    where = tile.reshape(1).astype(jnp.int32)
    states, class_map, perm_table, candidates, merge_rows = (
        pltpu.with_memory_space_constraint(value, pltpu.HBM)
        for value in (states, class_map, perm_table, candidates.reshape(128, 64), merge_order)
    )
    edge_shape, side_shape, states_shape = (131, 8, 128), (5, 8, 8, 128), (2, 64, 8, 8, 128)
    read_scratch = [pltpu.VMEM(CUBE, jnp.int32), pltpu.SMEM((8,), F32)]
    low, high = pl.pallas_call(
        edge_x_kernel,
        in_specs=[HBM, HBM, HBM],
        out_specs=[whole(edge_shape), whole(edge_shape)],
        out_shape=[jax.ShapeDtypeStruct(edge_shape, BF16), jax.ShapeDtypeStruct(edge_shape, BF16)],
        scratch_shapes=[pltpu.VMEM(states_shape, BF16)]
        + read_scratch
        + [pltpu.VMEM((129 * 64, 128), F32), pltpu.SemaphoreType.DMA((4,))],
        compiler_params=LIMIT,
    )(perm_table, class_map, states)

    def shift(value, axis, by):
        count = lax.axis_size(axis)
        return lax.ppermute(value, axis, [(i, (i + by) % count) for i in range(count)])

    from_low = shift(high, "gx", 1)
    from_high = shift(low, "gx", -1)

    side, perm, near_states, cells, hits = pl.pallas_call(
        edge_y_kernel,
        in_specs=[SMEM] + [HBM] * 5,
        out_specs=[whole(side_shape), whole(CUBE), whole(states_shape), whole((256, 128)), whole(CUBE)],
        out_shape=[
            jax.ShapeDtypeStruct(side_shape, BF16),
            jax.ShapeDtypeStruct(CUBE, F32),
            jax.ShapeDtypeStruct(states_shape, BF16),
            jax.ShapeDtypeStruct((256, 128), BF16),
            jax.ShapeDtypeStruct(CUBE, F32),
        ],
        scratch_shapes=[
            pltpu.VMEM(CUBE, jnp.int32),
            pltpu.VMEM((1, 64), jnp.int32),
            pltpu.VMEM((1, 128), jnp.int32),
            pltpu.SMEM((8,), F32),
            pltpu.SemaphoreType.DMA((6,)),
        ],
        compiler_params=LIMIT,
    )(where, perm_table, class_map, candidates, merge_rows, states)
    side_low = shift(side, "gy", 1)
    side_high = shift(side, "gy", -1)

    inner = pl.pallas_call(
        inner_kernel,
        in_specs=[whole(CUBE), whole(states_shape)],
        out_specs=whole((4096, 128)),
        out_shape=jax.ShapeDtypeStruct((4096, 128), F32),
        scratch_shapes=[
            pltpu.VMEM(CUBE, F32),
            pltpu.VMEM(FLAT, F32),
            pltpu.VMEM((7, 8, 128), F32),
            pltpu.VMEM((128, 128), BF16),
            pltpu.VMEM((256, 128), BF16),
        ],
        compiler_params=LIMIT,
    )(perm, near_states)
    numbers = lax.broadcasted_iota(jnp.int32, (63, 64, 128), 2)
    picks = (merge_order[64:, :64, None] == numbers).astype(BF16)
    inner, picks = lax.optimization_barrier((inner, picks))

    flux, mine_rows, send_rows = pl.pallas_call(
        outer_kernel,
        in_specs=[whole((4096, 128)), whole((256, 128)), whole(CUBE)]
        + [whole(edge_shape)] * 2 + [whole(side_shape)] + [whole(edge_shape)] * 2 + [whole(side_shape)] * 2,
        out_specs=[HBM, whole((32, 128)), whole((32, 128))],
        out_shape=[
            jax.ShapeDtypeStruct((64, 8, 8, 128), BF16),
            jax.ShapeDtypeStruct((32, 128), F32),
            jax.ShapeDtypeStruct((32, 128), F32),
        ],
        scratch_shapes=[
            pltpu.VMEM((4096, 128), F32),
            pltpu.VMEM((64, 8, 8, 128), BF16),
            pltpu.VMEM((2, 8, 128), F32),
            pltpu.VMEM((64, 256), BF16),
            pltpu.VMEM((256, 128), BF16),
            pltpu.VMEM((512, 128), F32),
            pltpu.SemaphoreType.DMA((2,)),
        ],
        compiler_params=LIMIT,
    )(inner, cells, hits, low, high, side, from_low, from_high, side_low, side_high)

    swap = [(i, i ^ 1) for i in range(8)]
    got_rows = lax.ppermute(send_rows, "gy", swap)
    merged = mine_rows[:, :64] + got_rows[:, :64]
    top = merged.astype(BF16)
    rest = (merged - lax.reduce_precision(merged, 8, 7)).astype(BF16)
    spread = jnp.broadcast_to(jnp.concatenate([top, rest], 1)[None], (64, 32, 128))
    peers = [[i * 8 + j * 2 + c for i in range(16) for j in range(4)] for c in range(2)]
    mine = lax.all_to_all(spread, ("gx", "gy"), 0, 0, axis_index_groups=peers)
    other = lax.ppermute(mine, "gy", swap)

    kept = pl.pallas_call(
        tree_kernel,
        in_specs=[SMEM, whole((63, 64, 128)), whole((64, 32, 128)), whole((64, 32, 128))],
        out_specs=HBM,
        out_shape=jax.ShapeDtypeStruct((64, 64, 127), F32),
        scratch_shapes=[
            pltpu.VMEM((63, 64, 128), BF16),
            pltpu.VMEM((128 * KEPT, 128), F32),
            pltpu.VMEM((64, 64, 127), F32),
            pltpu.VMEM((256, 128), BF16),
            pltpu.SemaphoreType.DMA((8,)),
        ],
        compiler_params=LIMIT,
    )(where, picks, mine, other)
    return flux, jnp.transpose(kept, (2, 0, 1))


def solution(mesh):
    in_specs = (P(None, None, None, "gx", "gy"), P(None, "gx", "gy"), P(), P(), P())
    out_specs = (P(None, None, "gx", "gy"), P())
    return jax.shard_map(local, mesh=mesh, in_specs=in_specs, out_specs=out_specs, check_vma=False)
```

```python
import jax
import jax.numpy as jnp
from jax import lax
from jax.experimental import pallas as pl
from jax.experimental.pallas import tpu as pltpu
from jax.sharding import PartitionSpec as P

F32 = jnp.float32
BF16 = jnp.bfloat16
KEPT = 72
UNROLL = 64
CUBE = (8, 8, 128)
FLAT = (64, 128)
EDGE = (131, 8, 128)
SIDE = (5, 8, 8, 128)
HBM = pl.BlockSpec(memory_space=pltpu.HBM)
SMEM = pl.BlockSpec(memory_space=pltpu.SMEM)
LIMIT = pltpu.CompilerParams(vmem_limit_bytes=48 * 1024 * 1024)


def whole(shape):
    return pl.BlockSpec(shape, lambda *_: (0,) * len(shape))


def lane_of(shape):
    return lax.broadcasted_iota(jnp.int32, shape, len(shape) - 1)


def turn(value, by):
    return pltpu.roll(value, by, 1)


def look_up(kind, table_ref):
    value = jnp.zeros(kind.shape, F32)
    for number in range(8):
        value = jnp.where(kind == number, table_ref[number], value)
    return value


def trans(k_here, k_next):
    return k_here * k_next / (k_here + k_next)


def face(t, m_here, m_next, p_here, p_next):
    return t * (m_here + m_next) * (p_next - p_here)


def three_pieces(value):
    high = value.astype(BF16)
    rest = value - high.astype(F32)
    middle = rest.astype(BF16)
    return high, middle, (rest - middle.astype(F32)).astype(BF16)


def edge_x_kernel(
    table_hbm, class_hbm, states_hbm, low_ref, high_ref, states_ref, class_ref, table_ref, wide_ref, sem
):
    copies = [
        pltpu.make_async_copy(table_hbm, table_ref, sem.at[0]),
        pltpu.make_async_copy(class_hbm, class_ref, sem.at[1]),
    ]
    for n, rows in enumerate((pl.ds(0, 2), pl.ds(6, 2))):
        copies.append(
            pltpu.make_async_copy(states_hbm.at[:, :, :, rows], states_ref.at[:, :, :, rows], sem.at[2 + n])
        )
    for copy in copies:
        copy.start()
    copies[0].wait()
    copies[1].wait()
    wide_ref[pl.ds(0, 64), :] = look_up(class_ref[...], table_ref).reshape(FLAT)
    for ref, at in ((low_ref, 0), (high_ref, 7)):
        for n, piece in enumerate(three_pieces(wide_ref[pl.ds(at, 8, stride=8), :])):
            ref[128 + n] = piece
    copies[2].wait()
    copies[3].wait()
    for snap in range(64):
        for field in range(2):
            slot = (1 + field + 2 * snap) * 64
            wide_ref[pl.ds(slot, 64), :] = states_ref[field, snap].astype(F32).reshape(FLAT)
            low_ref[field * 64 + snap] = wide_ref[pl.ds(slot, 8, stride=8), :].astype(BF16)
            high_ref[field * 64 + snap] = wide_ref[pl.ds(slot + 7, 8, stride=8), :].astype(BF16)


def two_times(weights):
    return jnp.concatenate([weights, weights], 0)


def two_pieces(value):
    high = value.astype(BF16)
    return jnp.concatenate([high, (value - high.astype(F32)).astype(BF16)], 1)


def matmul(left, right):
    return jnp.dot(left, right, preferred_element_type=F32)


def sub_of(shape):
    return lax.broadcasted_iota(jnp.int32, shape, 0)


def edge_y_kernel(
    where_ref, table_hbm, class_hbm, cand_hbm, order_hbm, states_hbm,
    side_ref, perm_ref, states_ref, cells_ref, hits_ref, class_ref, cand_ref, order_ref, table_ref, sem,
):
    tile = where_ref[0]
    core = tile % 2
    copies = [
        pltpu.make_async_copy(table_hbm, table_ref, sem.at[0]),
        pltpu.make_async_copy(class_hbm, class_ref, sem.at[1]),
        pltpu.make_async_copy(cand_hbm.at[pl.ds(tile, 1)], cand_ref, sem.at[2]),
        pltpu.make_async_copy(order_hbm.at[pl.ds(tile // 2, 1)], order_ref, sem.at[3]),
    ]
    for n in range(2):
        half = pl.ds(32 * n, 32)
        copies.append(pltpu.make_async_copy(states_hbm.at[:, half], states_ref.at[:, half], sem.at[4 + n]))
    for copy in copies:
        copy.start()
    for copy in copies[:4]:
        copy.wait()
    lane = lane_of(FLAT)
    order = jnp.broadcast_to(order_ref[...], FLAT)
    swapped = jnp.where(lane < 32, turn(order, 96), turn(order, 32))
    order = jnp.where(core == 1, swapped, order)
    match = (order == core * 64 + sub_of(FLAT)) & (lane < 64)
    column = jnp.transpose(jnp.broadcast_to(cand_ref[...].astype(F32), (64, 64)))[:, :1]
    cell = jnp.sum(jnp.where(match, jnp.broadcast_to(column, FLAT) + 1.0, 0.0), 0, keepdims=True)
    cell = cell.astype(jnp.int32) - 1
    at_y = jnp.where(cell < 0, -1, cell % 128)
    at_zx = jnp.where(cell < 0, -1, cell // 128)
    cells_ref[...] = two_times(jnp.where(sub_of((128, 128)) == at_y, 1.0, 0.0).astype(BF16))
    hits_ref[...] = jnp.where(sub_of(FLAT) == at_zx, 1.0, 0.0)

    perm = look_up(class_ref[...], table_ref)
    perm_ref[...] = perm
    first = jnp.broadcast_to(perm[:, :, 0:1], CUBE)
    last = jnp.broadcast_to(perm[:, :, 127:128], CUBE)
    for n, piece in enumerate(three_pieces(jnp.where(lane_of(CUBE) % 2 == 0, first, last))):
        side_ref[2 + n] = piece
    square = (128, 128)
    spread = jnp.where(sub_of(square) == jnp.where(lane_of(square) % 2 == 0, 0, 127), 1.0, 0.0).astype(BF16)
    acc = [jnp.zeros(FLAT, F32), jnp.zeros(FLAT, F32)]
    for snap in range(64):
        if snap % 32 == 0:
            copies[4 + snap // 32].wait()
        keep = (lane == 2 * snap) | (lane == (2 * snap + 127) % 128)
        for field in range(2):
            value = matmul(states_ref[field, snap].reshape(FLAT), spread)
            acc[field] = jnp.where(keep, value, acc[field])
    for field in range(2):
        side_ref[field] = acc[field].reshape(CUBE).astype(BF16)


def inner_kernel(perm_ref, states_ref, out_ref, tx_ref, ty_ref, tz_ref, shift_ref):
    perm = perm_ref[...]
    row = lax.broadcasted_iota(jnp.int32, CUBE, 1)
    next_y = turn(perm.reshape(FLAT), 127).reshape(CUBE)
    tx_ref[...] = jnp.where(row == 7, 0.0, trans(perm, jnp.roll(perm, -1, 1)))
    ty_ref[...] = jnp.where(lane_of(CUBE) == 127, 0.0, trans(perm, next_y)).reshape(FLAT)
    tz_ref[...] = trans(perm[:-1], perm[1:])
    square = (128, 128)
    shift_ref[...] = jnp.where(sub_of(square) == lane_of(square) + 1, 1.0, 0.0).astype(BF16)

    def group(number, carry):
        for k in range(16):
            snap = number * 16 + k
            p = states_ref[0, snap].astype(F32)
            s = states_ref[1, snap].astype(F32)
            m = s * s
            fx = face(tx_ref[...], m, jnp.roll(m, -1, 1), p, jnp.roll(p, -1, 1))
            total = fx - jnp.roll(fx, 1, 1)
            p_next = matmul(states_ref[0, snap].reshape(FLAT), shift_ref[...])
            s_next = matmul(states_ref[1, snap].reshape(FLAT), shift_ref[...])
            fy = face(ty_ref[...], m.reshape(FLAT), s_next * s_next, p.reshape(FLAT), p_next)
            total = total + (fy - turn(fy, 1)).reshape(CUBE)
            fz = face(tz_ref[...], m[:-1], m[1:], p[:-1], p[1:])
            zero = jnp.zeros((1, 8, 128), F32)
            total = total + (jnp.concatenate([fz, zero], 0) - jnp.concatenate([zero, fz], 0))
            out_ref[pl.ds(pl.multiple_of(snap * 64, 64), 64), :] = total.reshape(FLAT)
        return carry

    lax.fori_loop(0, 4, group, 0)


def sum_of_eights(picked_ref):
    total = picked_ref[pl.ds(0, 64, stride=8), :]
    for at in range(1, 8):
        total = total + picked_ref[pl.ds(at, 64, stride=8), :]
    return total


def perm_of(ref, at):
    high, middle, low = (ref[at + n].astype(F32) for n in range(3))
    return (high + middle) + low


def middle_kernel(
    inner_ref, cells_ref, hits_ref, side_ref, side_low_ref, side_high_ref, flux_ref, rows_ref, qy_ref, picked_ref
):
    lane = lane_of(FLAT)

    def beyond(below, above):
        below, above = below.reshape(FLAT), above.reshape(FLAT)
        return jnp.where(lane % 2 == 0, turn(below, 1), turn(above, 127))

    t_side = trans(
        perm_of(side_ref, 2).reshape(FLAT), beyond(perm_of(side_low_ref, 2), perm_of(side_high_ref, 2))
    )

    def side_pair(which):
        here = side_ref[which].astype(F32).reshape(FLAT)
        return here, beyond(side_low_ref[which].astype(F32), side_high_ref[which].astype(F32))

    p_here, p_next = side_pair(0)
    s_here, s_next = side_pair(1)
    qy_ref[...] = face(t_side, s_here * s_here, s_next * s_next, p_here, p_next)
    at_edge = (lane == 0) | (lane == 127)

    def group(number, carry):
        for k in range(UNROLL):
            snap = number * UNROLL + k
            span = pl.ds(pl.multiple_of(snap * 64, 64), 64)
            turned = turn(qy_ref[...], (128 - 2 * snap) % 128)
            flux = inner_ref[span, :] + jnp.where(at_edge, turned, 0.0)
            flux_ref[span, :] = flux
            rows = matmul(two_pieces(flux), cells_ref[...]) * hits_ref[...]
            picked_ref[pl.ds(pl.multiple_of(snap * 8, 8), 8), :] = jnp.sum(rows.reshape(CUBE), 0)
        return carry

    lax.fori_loop(0, 64 // UNROLL, group, 0)
    rows_ref[...] = sum_of_eights(picked_ref)


def outer_kernel(
    within_ref, rows_ref, cells_ref, hits_ref, low_ref, high_ref, from_low_ref, from_high_ref,
    out_hbm, mine_ref, send_ref, out_ref, edge_ref, qx_ref, picked_ref, sem,
):
    t_low = trans(perm_of(low_ref, 128), perm_of(from_low_ref, 128))
    t_high = trans(perm_of(high_ref, 128), perm_of(from_high_ref, 128))
    edge_ref[...] = jnp.zeros_like(edge_ref)

    def edge(own_ref, other_ref, t, snap):
        s_here, s_next = own_ref[64 + snap].astype(F32), other_ref[64 + snap].astype(F32)
        p_here, p_next = own_ref[snap].astype(F32), other_ref[snap].astype(F32)
        return face(t, s_here * s_here, s_next * s_next, p_here, p_next)

    def put(part):
        span = pl.ds(part * 32, 32)
        return pltpu.make_async_copy(out_ref.at[span], out_hbm.at[span], sem.at[part])

    def group(number, carry):
        for k in range(16):
            snap = number * 16 + k
            q_low = edge(low_ref, from_low_ref, t_low, snap)
            q_high = edge(high_ref, from_high_ref, t_high, snap)
            at = pl.multiple_of(snap * 16, 16)
            qx_ref[pl.ds(at, 8), :] = q_low
            qx_ref[pl.ds(at + 8, 8), :] = q_high
            edge_ref[pl.ds(k * 64, 8, stride=8), :] = q_low
            edge_ref[pl.ds(k * 64 + 7, 8, stride=8), :] = q_high
        for k in range(16):
            snap = number * 16 + k
            flux = within_ref[pl.ds(pl.multiple_of(snap * 64, 64), 64), :] + edge_ref[pl.ds(k * 64, 64), :]
            out_ref[snap] = flux.reshape(CUBE).astype(BF16)
        return carry

    for part in range(2):
        lax.fori_loop(2 * part, 2 * part + 2, group, 0)
        put(part).start()

    hit_low, hit_high = hits_ref[pl.ds(0, 8, stride=8), :], hits_ref[pl.ds(7, 8, stride=8), :]
    for part in range(4):
        rows = matmul(two_pieces(qx_ref[pl.ds(part * 256, 256), :]), cells_ref[...])
        for k in range(16):
            low = rows[k * 16 : k * 16 + 8] * hit_low
            high = rows[k * 16 + 8 : k * 16 + 16] * hit_high
            picked_ref[pl.ds((part * 16 + k) * 8, 8), :] = low + high
    total = rows_ref[...] + sum_of_eights(picked_ref)
    rows = jnp.transpose(jnp.concatenate([total, jnp.zeros(FLAT, F32)], 0))
    mine_ref[...] = rows[:32]
    send_ref[...] = rows[32:64]
    for part in range(2):
        put(part).wait()


def tree_kernel(where_ref, pick_ref, mine_ref, other_ref, out_hbm, level_ref, kept_ref, out_ref, sem):
    def select(node, stack):
        got = matmul(pick_ref[node - 64], stack)
        kept_ref[pl.ds(node * KEPT, 64), :] = got
        level_ref[node - 64] = got.astype(BF16)

    def first_levels(low_ref, high_ref):
        for j in range(32):
            pair = [low_ref[2 * j], high_ref[2 * j], low_ref[2 * j + 1], high_ref[2 * j + 1]]
            select(64 + j, jnp.concatenate(pair, 0))
        for chip in range(64):
            kept_ref[pl.ds(chip * KEPT, 32), :] = low_ref[chip].astype(F32)
            kept_ref[pl.ds(chip * KEPT + 32, 32), :] = high_ref[chip].astype(F32)

    @pl.when(where_ref[0] % 2 == 0)
    def _():
        first_levels(mine_ref, other_ref)

    @pl.when(where_ref[0] % 2 == 1)
    def _():
        first_levels(other_ref, mine_ref)

    before, offset, count = 64, 96, 16
    while count >= 1:
        for j in range(count):
            select(offset + j, level_ref[pl.ds(before + 2 * j - 64, 2)].reshape(128, 128))
        before, offset, count = offset, offset + count, count // 2

    def put(at):
        span = pl.ds(at, 16)
        return pltpu.make_async_copy(out_ref.at[span], out_hbm.at[span], sem.at[at // 16])

    for slot in range(64):
        turned = jnp.transpose(kept_ref[pl.ds(slot, 128, stride=KEPT), :])
        out_ref[slot] = (turned[:64] + turned[64:])[:, :127]
        if slot % 16 == 15:
            put(slot - 15).start()
    for at in range(0, 64, 16):
        put(at).wait()


def middle_call(*operands):
    return pl.pallas_call(
        middle_kernel,
        in_specs=[whole((4096, 128)), whole((256, 128)), whole(FLAT), whole(SIDE), whole(SIDE), whole(SIDE)],
        out_specs=[whole((4096, 128)), whole(FLAT)],
        out_shape=[jax.ShapeDtypeStruct((4096, 128), F32), jax.ShapeDtypeStruct(FLAT, F32)],
        scratch_shapes=[pltpu.VMEM(FLAT, F32), pltpu.VMEM((512, 128), F32)],
        compiler_params=LIMIT,
    )(*operands)


def outer_call(*operands):
    return pl.pallas_call(
        outer_kernel,
        in_specs=[whole((4096, 128)), whole(FLAT), whole((256, 128)), whole(FLAT)] + [whole(EDGE)] * 4,
        out_specs=[HBM, whole((32, 128)), whole((32, 128))],
        out_shape=[
            jax.ShapeDtypeStruct((64, 8, 8, 128), BF16),
            jax.ShapeDtypeStruct((32, 128), F32),
            jax.ShapeDtypeStruct((32, 128), F32),
        ],
        scratch_shapes=[
            pltpu.VMEM((64, 8, 8, 128), BF16),
            pltpu.VMEM((1024, 128), F32),
            pltpu.VMEM((1024, 128), F32),
            pltpu.VMEM((512, 128), F32),
            pltpu.SemaphoreType.DMA((2,)),
        ],
        compiler_params=LIMIT,
    )(*operands)


def tree_call(*operands):
    return pl.pallas_call(
        tree_kernel,
        in_specs=[SMEM, whole((63, 64, 128)), whole((64, 32, 128)), whole((64, 32, 128))],
        out_specs=HBM,
        out_shape=jax.ShapeDtypeStruct((64, 64, 127), F32),
        scratch_shapes=[
            pltpu.VMEM((63, 64, 128), BF16),
            pltpu.VMEM((128 * KEPT, 128), F32),
            pltpu.VMEM((64, 64, 127), F32),
            pltpu.SemaphoreType.DMA((4,)),
        ],
        compiler_params=LIMIT,
    )(*operands)


def local(states, class_map, perm_table, candidates, merge_order):
    tile = lax.axis_index("gx") * lax.axis_size("gy") + lax.axis_index("gy")
    where = tile.reshape(1).astype(jnp.int32)
    states, class_map, perm_table, candidates, merge_rows = (
        pltpu.with_memory_space_constraint(value, pltpu.HBM)
        for value in (states, class_map, perm_table, candidates.reshape(128, 64), merge_order)
    )
    states_shape = (2, 64, 8, 8, 128)
    read_scratch = [pltpu.VMEM(CUBE, jnp.int32), pltpu.SMEM((8,), F32)]
    low, high = pl.pallas_call(
        edge_x_kernel,
        in_specs=[HBM, HBM, HBM],
        out_specs=[whole(EDGE), whole(EDGE)],
        out_shape=[jax.ShapeDtypeStruct(EDGE, BF16), jax.ShapeDtypeStruct(EDGE, BF16)],
        scratch_shapes=[pltpu.VMEM(states_shape, BF16)]
        + read_scratch
        + [pltpu.VMEM((129 * 64, 128), F32), pltpu.SemaphoreType.DMA((4,))],
        compiler_params=LIMIT,
    )(perm_table, class_map, states)

    def shift(value, axis, by):
        count = lax.axis_size(axis)
        return lax.ppermute(value, axis, [(i, (i + by) % count) for i in range(count)])

    from_low = shift(high, "gx", 1)
    from_high = shift(low, "gx", -1)

    side, perm, near_states, cells, hits = pl.pallas_call(
        edge_y_kernel,
        in_specs=[SMEM] + [HBM] * 5,
        out_specs=[whole(SIDE), whole(CUBE), whole(states_shape), whole((256, 128)), whole(FLAT)],
        out_shape=[
            jax.ShapeDtypeStruct(SIDE, BF16),
            jax.ShapeDtypeStruct(CUBE, F32),
            jax.ShapeDtypeStruct(states_shape, BF16),
            jax.ShapeDtypeStruct((256, 128), BF16),
            jax.ShapeDtypeStruct(FLAT, F32),
        ],
        scratch_shapes=[
            pltpu.VMEM(CUBE, jnp.int32),
            pltpu.VMEM((1, 64), jnp.int32),
            pltpu.VMEM((1, 128), jnp.int32),
            pltpu.SMEM((8,), F32),
            pltpu.SemaphoreType.DMA((6,)),
        ],
        compiler_params=LIMIT,
    )(where, perm_table, class_map, candidates, merge_rows, states)
    side_low = shift(side, "gy", 1)
    side_high = shift(side, "gy", -1)

    inner = pl.pallas_call(
        inner_kernel,
        in_specs=[whole(CUBE), whole(states_shape)],
        out_specs=whole((4096, 128)),
        out_shape=jax.ShapeDtypeStruct((4096, 128), F32),
        scratch_shapes=[
            pltpu.VMEM(CUBE, F32),
            pltpu.VMEM(FLAT, F32),
            pltpu.VMEM((7, 8, 128), F32),
            pltpu.VMEM((128, 128), BF16),
        ],
        compiler_params=LIMIT,
    )(perm, near_states)
    numbers = lax.broadcasted_iota(jnp.int32, (63, 64, 128), 2)
    picks = (merge_order[64:, :64, None] == numbers).astype(BF16)
    inner, picks = lax.optimization_barrier((inner, picks))

    within, part_rows = middle_call(inner, cells, hits, side, side_low, side_high)
    flux, mine_rows, send_rows = outer_call(within, part_rows, cells, hits, low, high, from_low, from_high)

    swap = [(i, i ^ 1) for i in range(8)]
    got_rows = lax.ppermute(send_rows, "gy", swap)
    merged = mine_rows[:, :64] + got_rows[:, :64]
    top = merged.astype(BF16)
    rest = (merged - lax.reduce_precision(merged, 8, 7)).astype(BF16)
    spread = jnp.broadcast_to(jnp.concatenate([top, rest], 1)[None], (64, 32, 128))
    peers = [[i * 8 + j * 2 + c for i in range(16) for j in range(4)] for c in range(2)]
    mine = lax.all_to_all(spread, ("gx", "gy"), 0, 0, axis_index_groups=peers)
    other = lax.ppermute(mine, "gy", swap)

    kept = tree_call(where, picks, mine, other)
    return flux, jnp.transpose(kept, (2, 0, 1))


def solution(mesh):
    in_specs = (P(None, None, None, "gx", "gy"), P(None, "gx", "gy"), P(), P(), P())
    out_specs = (P(None, None, "gx", "gy"), P())
    return jax.shard_map(local, mesh=mesh, in_specs=in_specs, out_specs=out_specs, check_vma=False)
```

```python
import jax
import jax.numpy as jnp
from jax import lax
from jax.experimental import pallas as pl
from jax.experimental.pallas import tpu as pltpu
from jax.sharding import PartitionSpec as P

F32 = jnp.float32
BF16 = jnp.bfloat16
KEPT = 72
CUBE = (8, 8, 128)
FLAT = (64, 128)
EDGE = (131, 8, 128)
SIDE = (5, 8, 8, 128)
HBM = pl.BlockSpec(memory_space=pltpu.HBM)
SMEM = pl.BlockSpec(memory_space=pltpu.SMEM)
LIMIT = pltpu.CompilerParams(vmem_limit_bytes=32 * 1024 * 1024)


def whole(shape):
    return pl.BlockSpec(shape, lambda *_: (0,) * len(shape))


def lane_of(shape):
    return lax.broadcasted_iota(jnp.int32, shape, len(shape) - 1)


def turn(value, by):
    return pltpu.roll(value, by, 1)


def look_up(kind, table_ref):
    value = jnp.zeros(kind.shape, F32)
    for number in range(8):
        value = jnp.where(kind == number, table_ref[number], value)
    return value


def trans(k_here, k_next):
    return k_here * k_next / (k_here + k_next)


def face(t, m_here, m_next, p_here, p_next):
    return t * (m_here + m_next) * (p_next - p_here)


def three_pieces(value):
    high = value.astype(BF16)
    rest = value - high.astype(F32)
    middle = rest.astype(BF16)
    return high, middle, (rest - middle.astype(F32)).astype(BF16)


def two_times(weights):
    return jnp.concatenate([weights, weights], 0)


def two_pieces(value):
    high = value.astype(BF16)
    return jnp.concatenate([high, (value - high.astype(F32)).astype(BF16)], 1)


def matmul(left, right):
    return jnp.dot(left, right, preferred_element_type=F32)


def sub_of(shape):
    return lax.broadcasted_iota(jnp.int32, shape, 0)


def slots_of(order_row, cand_row, core):
    lane = lane_of(FLAT)
    order = jnp.broadcast_to(order_row, FLAT)
    swapped = jnp.where(lane < 32, turn(order, 96), turn(order, 32))
    order = jnp.where(core == 1, swapped, order)
    match = (order == core * 64 + sub_of(FLAT)) & (lane < 64)
    column = jnp.transpose(jnp.broadcast_to(cand_row.astype(F32), (64, 64)))[:, :1]
    cell = jnp.sum(jnp.where(match, jnp.broadcast_to(column, FLAT) + 1.0, 0.0), 0, keepdims=True)
    cell = cell.astype(jnp.int32) - 1
    return jnp.where(cell < 0, -1, cell % 128), jnp.where(cell < 0, -1, cell // 128)


def one_hot(shape, at):
    return jnp.where(sub_of(shape) == at, 1.0, 0.0)


def edge_x_kernel(
    where_ref, table_hbm, class_hbm, cand_hbm, order_hbm, states_hbm,
    low_ref, high_ref, to_minus_ref, to_plus_ref, own_ref, cells_ref, hits_ref,
    states_ref, class_ref, cand_ref, order_ref, table_ref, wide_ref, weights_ref, product_ref, sem,
):
    tile = where_ref[0]
    core = tile % 2
    tiles = (tile, (tile + 120) % 128, (tile + 8) % 128)
    copies = [
        pltpu.make_async_copy(table_hbm, table_ref, sem.at[0]),
        pltpu.make_async_copy(class_hbm, class_ref, sem.at[1]),
    ]
    for n, at in enumerate(tiles):
        copies.append(pltpu.make_async_copy(cand_hbm.at[pl.ds(at, 1)], cand_ref.at[n], sem.at[2 + n]))
        copies.append(pltpu.make_async_copy(order_hbm.at[pl.ds(at // 2, 1)], order_ref.at[n], sem.at[5 + n]))
    for n, rows in enumerate((pl.ds(0, 2), pl.ds(6, 2))):
        copies.append(
            pltpu.make_async_copy(states_hbm.at[:, :, :, rows], states_ref.at[:, :, :, rows], sem.at[8 + n])
        )
    for copy in copies:
        copy.start()
    for copy in copies[:8]:
        copy.wait()
    wide_ref[pl.ds(0, 64), :] = look_up(class_ref[...], table_ref).reshape(FLAT)
    for ref, at in ((low_ref, 0), (high_ref, 7)):
        for n, piece in enumerate(three_pieces(wide_ref[pl.ds(at, 8, stride=8), :])):
            ref[128 + n] = piece
    own_y, own_zx = slots_of(order_ref[0], cand_ref[0], core)
    minus_y, minus_zx = slots_of(order_ref[1], cand_ref[1], core)
    plus_y, plus_zx = slots_of(order_ref[2], cand_ref[2], core)
    square, rows_of_z = (128, 128), (8, 128)
    own_cells = one_hot(square, own_y).astype(BF16)
    cells_ref[...] = two_times(own_cells)
    hits_ref[...] = one_hot(FLAT, own_zx)
    weights_ref[0] = jnp.concatenate([one_hot(square, minus_y).astype(BF16), own_cells], 1)
    weights_ref[1] = jnp.concatenate([one_hot(square, plus_y).astype(BF16), own_cells], 1)
    own_z = sub_of(rows_of_z) * 8
    mask_low = jnp.concatenate(
        [one_hot(rows_of_z, jnp.where(minus_zx < 0, -1, minus_zx // 8)), jnp.where(own_z == own_zx, 1.0, 0.0)], 1
    )
    mask_high = jnp.concatenate(
        [one_hot(rows_of_z, jnp.where(plus_zx < 0, -1, plus_zx // 8)), jnp.where(own_z + 7 == own_zx, 1.0, 0.0)], 1
    )
    at_low = jnp.where((own_zx >= 0) & (own_zx % 8 == 0), 1.0, 0.0)
    at_high = jnp.where((own_zx >= 0) & (own_zx % 8 == 7), 1.0, 0.0)
    flag = sub_of(rows_of_z)
    flags = jnp.where(flag == 0, at_low, jnp.where(flag == 1, at_high, 0.0))
    copies[8].wait()
    copies[9].wait()
    for snap in range(64):
        for field in range(2):
            slot = (1 + field + 2 * snap) * 64
            wide_ref[pl.ds(slot, 64), :] = states_ref[field, snap].astype(F32).reshape(FLAT)
            low_ref[field * 64 + snap] = wide_ref[pl.ds(slot, 8, stride=8), :].astype(BF16)
            high_ref[field * 64 + snap] = wide_ref[pl.ds(slot + 7, 8, stride=8), :].astype(BF16)

    def select(ref, weights, mask):
        for first, count in [(16 * n, 16) for n in range(8)] + [(128, 3)]:
            rows = matmul(ref[pl.ds(first, count)].reshape(count * 8, 128), weights)
            for n in range(count):
                product = rows[n * 8 : n * 8 + 8] * mask
                for half in range(2):
                    product_ref[half, pl.ds((first + n) * 8, 8), :] = product[:, half * 128 : half * 128 + 128]
        halves = []
        for half in range(2):
            product_ref[half, pl.ds(131 * 8, 40), :] = jnp.zeros((40, 128), F32)
            total = product_ref[half, pl.ds(0, 136, stride=8), :]
            for z in range(1, 8):
                total = total + product_ref[half, pl.ds(z, 136, stride=8), :]
            halves.append(total)
        return halves

    def pack(rows):
        return jnp.concatenate([rows[:64] + turn(rows[64:128], 64), rows[128:136]], 0).astype(BF16)

    to_minus, own_low = select(low_ref, weights_ref[0], mask_low)
    to_plus, own_high = select(high_ref, weights_ref[1], mask_high)
    to_minus_ref[...] = pack(to_minus)
    to_plus_ref[...] = pack(to_plus)
    own_ref[pl.ds(0, 136), :] = own_low + own_high
    own_ref[pl.ds(136, 8), :] = flags


def edge_y_kernel(table_hbm, class_hbm, states_hbm, side_ref, perm_ref, states_ref, class_ref, table_ref, sem):
    copies = [
        pltpu.make_async_copy(table_hbm, table_ref, sem.at[0]),
        pltpu.make_async_copy(class_hbm, class_ref, sem.at[1]),
    ]
    for n in range(2):
        half = pl.ds(32 * n, 32)
        copies.append(pltpu.make_async_copy(states_hbm.at[:, half], states_ref.at[:, half], sem.at[2 + n]))
    for copy in copies:
        copy.start()
    copies[0].wait()
    copies[1].wait()
    perm = look_up(class_ref[...], table_ref)
    perm_ref[...] = perm
    first = jnp.broadcast_to(perm[:, :, 0:1], CUBE)
    last = jnp.broadcast_to(perm[:, :, 127:128], CUBE)
    for n, piece in enumerate(three_pieces(jnp.where(lane_of(CUBE) % 2 == 0, first, last))):
        side_ref[2 + n] = piece
    lane = lane_of(FLAT)
    acc = [jnp.zeros(FLAT, F32), jnp.zeros(FLAT, F32)]
    for snap in range(64):
        if snap % 32 == 0:
            copies[2 + snap // 32].wait()
        keep = (lane == 2 * snap) | (lane == (2 * snap + 127) % 128)
        for field in range(2):
            value = states_ref[field, snap].astype(F32).reshape(FLAT)
            acc[field] = jnp.where(keep, turn(value, 2 * snap), acc[field])
    for field in range(2):
        side_ref[field] = acc[field].reshape(CUBE).astype(BF16)


def set_up_faces(perm, tx_ref, ty_ref, tz_ref, shift_ref):
    row = lax.broadcasted_iota(jnp.int32, CUBE, 1)
    next_y = turn(perm.reshape(FLAT), 127).reshape(CUBE)
    tx_ref[...] = jnp.where(row == 7, 0.0, trans(perm, jnp.roll(perm, -1, 1)))
    ty_ref[...] = jnp.where(lane_of(CUBE) == 127, 0.0, trans(perm, next_y)).reshape(FLAT)
    tz_ref[...] = trans(perm[:-1], perm[1:])
    square = (128, 128)
    shift_ref[...] = jnp.where(sub_of(square) == lane_of(square) + 1, 1.0, 0.0).astype(BF16)


def flux_within(states_ref, snap, tx_ref, ty_ref, tz_ref, shift_ref):
    p = states_ref[0, snap].astype(F32)
    s = states_ref[1, snap].astype(F32)
    m = s * s
    fx = face(tx_ref[...], m, jnp.roll(m, -1, 1), p, jnp.roll(p, -1, 1))
    total = fx - jnp.roll(fx, 1, 1)
    p_next = matmul(states_ref[0, snap].reshape(FLAT), shift_ref[...])
    s_next = matmul(states_ref[1, snap].reshape(FLAT), shift_ref[...])
    fy = face(ty_ref[...], m.reshape(FLAT), s_next * s_next, p.reshape(FLAT), p_next)
    total = total + (fy - turn(fy, 1)).reshape(CUBE)
    fz = face(tz_ref[...], m[:-1], m[1:], p[:-1], p[1:])
    zero = jnp.zeros((1, 8, 128), F32)
    total = total + (jnp.concatenate([fz, zero], 0) - jnp.concatenate([zero, fz], 0))
    return total.reshape(FLAT)


def inner_kernel(perm_ref, states_ref, out_ref, tx_ref, ty_ref, tz_ref, shift_ref):
    faces = (tx_ref, ty_ref, tz_ref, shift_ref)
    set_up_faces(perm_ref[...], *faces)

    def group(number, carry):
        for k in range(16):
            snap = number * 16 + k
            span = pl.ds(pl.multiple_of(snap * 64, 64), 64)
            out_ref[span, :] = flux_within(states_ref, snap, *faces)
        return carry

    lax.fori_loop(0, 4, group, 0)


def sum_of_eights(picked_ref):
    total = picked_ref[pl.ds(0, 64, stride=8), :]
    for at in range(1, 8):
        total = total + picked_ref[pl.ds(at, 64, stride=8), :]
    return total


def perm_of(ref, at):
    high, middle, low = (ref[at + n].astype(F32) for n in range(3))
    return (high + middle) + low


def flux_across_y(side_ref, side_low_ref, side_high_ref):
    lane = lane_of(FLAT)

    def beyond(below, above):
        below, above = below.reshape(FLAT), above.reshape(FLAT)
        return jnp.where(lane % 2 == 0, turn(below, 1), turn(above, 127))

    t_side = trans(
        perm_of(side_ref, 2).reshape(FLAT), beyond(perm_of(side_low_ref, 2), perm_of(side_high_ref, 2))
    )

    def side_pair(which):
        here = side_ref[which].astype(F32).reshape(FLAT)
        return here, beyond(side_low_ref[which].astype(F32), side_high_ref[which].astype(F32))

    p_here, p_next = side_pair(0)
    s_here, s_next = side_pair(1)
    return face(t_side, s_here * s_here, s_next * s_next, p_here, p_next)


def sides_of(qy_ref, snap):
    lane = lane_of(FLAT)
    turned = turn(qy_ref[...], (128 - 2 * snap) % 128)
    return jnp.where((lane == 0) | (lane == 127), turned, 0.0)


def middle_kernel(
    inner_ref, cells_ref, hits_ref, side_ref, side_low_ref, side_high_ref, own_ref, from_minus_ref, from_plus_ref,
    mine_ref, send_ref, qy_ref, picked_ref,
):
    qy_ref[...] = flux_across_y(side_ref, side_low_ref, side_high_ref)
    for snap in range(64):
        flux = inner_ref[pl.ds(snap * 64, 64), :] + sides_of(qy_ref, snap)
        rows = matmul(two_pieces(flux), cells_ref[...]) * hits_ref[...]
        picked_ref[pl.ds(snap * 8, 8), :] = jnp.sum(rows.reshape(CUBE), 0)
    at_low, at_high = own_ref[pl.ds(136, 1), :], own_ref[pl.ds(137, 1), :]
    beside = from_minus_ref[...].astype(F32) * at_low + from_plus_ref[...].astype(F32) * at_high
    sat = from_minus_ref[:64].astype(F32) * turn(at_low, 64) + from_plus_ref[:64].astype(F32) * turn(at_high, 64)
    m_next, p_next = turn(sat, 64), beside[:64]
    p_own, m_own = own_ref[pl.ds(0, 64), :], own_ref[pl.ds(64, 64), :]
    k_next = (beside[64:65] + beside[65:66]) + beside[66:67]
    k_own = (own_ref[pl.ds(128, 1), :] + own_ref[pl.ds(129, 1), :]) + own_ref[pl.ds(130, 1), :]
    k_sum = jnp.where(at_low + at_high > 0.0, k_own + k_next, 1.0)
    q_x = face(k_own * k_next / k_sum, m_own * m_own, m_next * m_next, p_own, p_next)
    total = sum_of_eights(picked_ref) + q_x
    rows = jnp.transpose(jnp.concatenate([total, jnp.zeros(FLAT, F32)], 0))
    mine_ref[...] = rows[:32]
    send_ref[...] = rows[32:64]


def near_kernel(
    perm_ref, side_ref, side_low_ref, side_high_ref, states_hbm, out_ref,
    states_ref, tx_ref, ty_ref, tz_ref, shift_ref, qy_ref, sem,
):
    copies = []
    for n in range(2):
        half = pl.ds(32 * n, 32)
        copies.append(pltpu.make_async_copy(states_hbm.at[:, half], states_ref.at[:, half], sem.at[n]))
        copies[n].start()
    faces = (tx_ref, ty_ref, tz_ref, shift_ref)
    set_up_faces(perm_ref[...], *faces)
    qy_ref[...] = flux_across_y(side_ref, side_low_ref, side_high_ref)

    def group(number, carry):
        for k in range(16):
            snap = number * 16 + k
            span = pl.ds(pl.multiple_of(snap * 64, 64), 64)
            out_ref[span, :] = flux_within(states_ref, snap, *faces) + sides_of(qy_ref, snap)
        return carry

    for n in range(2):
        copies[n].wait()
        lax.fori_loop(2 * n, 2 * n + 2, group, 0)


def outer_kernel(within_ref, low_ref, high_ref, from_low_ref, from_high_ref, out_hbm, out_ref, edge_ref, sem):
    t_low = trans(perm_of(low_ref, 128), perm_of(from_low_ref, 128))
    t_high = trans(perm_of(high_ref, 128), perm_of(from_high_ref, 128))
    edge_ref[...] = jnp.zeros_like(edge_ref)

    def edge(own_ref, other_ref, t, snap):
        s_here, s_next = own_ref[64 + snap].astype(F32), other_ref[64 + snap].astype(F32)
        p_here, p_next = own_ref[snap].astype(F32), other_ref[snap].astype(F32)
        return face(t, s_here * s_here, s_next * s_next, p_here, p_next)

    def put(part):
        span = pl.ds(part * 32, 32)
        return pltpu.make_async_copy(out_ref.at[span], out_hbm.at[span], sem.at[part])

    def group(number, carry):
        for k in range(16):
            snap = number * 16 + k
            edge_ref[pl.ds(k * 64, 8, stride=8), :] = edge(low_ref, from_low_ref, t_low, snap)
            edge_ref[pl.ds(k * 64 + 7, 8, stride=8), :] = edge(high_ref, from_high_ref, t_high, snap)
        for k in range(16):
            snap = number * 16 + k
            flux = within_ref[pl.ds(pl.multiple_of(snap * 64, 64), 64), :] + edge_ref[pl.ds(k * 64, 64), :]
            out_ref[snap] = flux.reshape(CUBE).astype(BF16)
        return carry

    for part in range(2):
        lax.fori_loop(2 * part, 2 * part + 2, group, 0)
        put(part).start()
    for part in range(2):
        put(part).wait()


def tree_kernel(where_ref, pick_ref, mine_ref, other_ref, out_hbm, level_ref, kept_ref, out_ref, sem):
    def select(node, stack):
        got = matmul(pick_ref[node - 64], stack)
        kept_ref[pl.ds(node * KEPT, 64), :] = got
        level_ref[node - 64] = got.astype(BF16)

    def first_levels(low_ref, high_ref):
        for j in range(32):
            pair = [low_ref[2 * j], high_ref[2 * j], low_ref[2 * j + 1], high_ref[2 * j + 1]]
            select(64 + j, jnp.concatenate(pair, 0))
        for chip in range(64):
            kept_ref[pl.ds(chip * KEPT, 32), :] = low_ref[chip].astype(F32)
            kept_ref[pl.ds(chip * KEPT + 32, 32), :] = high_ref[chip].astype(F32)

    @pl.when(where_ref[0] % 2 == 0)
    def _():
        first_levels(mine_ref, other_ref)

    @pl.when(where_ref[0] % 2 == 1)
    def _():
        first_levels(other_ref, mine_ref)

    before, offset, count = 64, 96, 16
    while count >= 1:
        for j in range(count):
            select(offset + j, level_ref[pl.ds(before + 2 * j - 64, 2)].reshape(128, 128))
        before, offset, count = offset, offset + count, count // 2

    def put(at):
        span = pl.ds(at, 16)
        return pltpu.make_async_copy(out_ref.at[span], out_hbm.at[span], sem.at[at // 16])

    for slot in range(64):
        turned = jnp.transpose(kept_ref[pl.ds(slot, 128, stride=KEPT), :])
        out_ref[slot] = (turned[:64] + turned[64:])[:, :127]
        if slot % 16 == 15:
            put(slot - 15).start()
    for at in range(0, 64, 16):
        put(at).wait()


ROWS = jax.ShapeDtypeStruct((32, 128), F32)
SLOTS = (72, 128)
OWN = (144, 128)


def edge_x_call(*operands):
    edge, slots = jax.ShapeDtypeStruct(EDGE, BF16), jax.ShapeDtypeStruct(SLOTS, BF16)
    shapes = [
        edge, edge, slots, slots, jax.ShapeDtypeStruct(OWN, F32),
        jax.ShapeDtypeStruct((256, 128), BF16), jax.ShapeDtypeStruct(FLAT, F32),
    ]
    return pl.pallas_call(
        edge_x_kernel,
        in_specs=[SMEM] + [HBM] * 5,
        out_specs=[whole(one.shape) for one in shapes],
        out_shape=shapes,
        scratch_shapes=[
            pltpu.VMEM((2, 64, 8, 8, 128), BF16),
            pltpu.VMEM(CUBE, jnp.int32),
            pltpu.VMEM((3, 1, 64), jnp.int32),
            pltpu.VMEM((3, 1, 128), jnp.int32),
            pltpu.SMEM((8,), F32),
            pltpu.VMEM((129 * 64, 128), F32),
            pltpu.VMEM((2, 128, 256), BF16),
            pltpu.VMEM((2, 136 * 8, 128), F32),
            pltpu.SemaphoreType.DMA((10,)),
        ],
        compiler_params=LIMIT,
    )(*operands)


def middle_call(*operands):
    return pl.pallas_call(
        middle_kernel,
        in_specs=[whole((4096, 128)), whole((256, 128)), whole(FLAT)]
        + [whole(SIDE)] * 3 + [whole(OWN), whole(SLOTS), whole(SLOTS)],
        out_specs=[whole((32, 128)), whole((32, 128))],
        out_shape=[ROWS, ROWS],
        scratch_shapes=[pltpu.VMEM(FLAT, F32), pltpu.VMEM((512, 128), F32)],
        compiler_params=LIMIT,
    )(*operands)


FACES = [
    pltpu.VMEM(CUBE, F32), pltpu.VMEM(FLAT, F32), pltpu.VMEM((7, 8, 128), F32), pltpu.VMEM((128, 128), BF16)
]


def near_call(*operands):
    return pl.pallas_call(
        near_kernel,
        in_specs=[whole(CUBE)] + [whole(SIDE)] * 3 + [HBM],
        out_specs=whole((4096, 128)),
        out_shape=jax.ShapeDtypeStruct((4096, 128), F32),
        scratch_shapes=[pltpu.VMEM((2, 64, 8, 8, 128), BF16)]
        + FACES
        + [pltpu.VMEM(FLAT, F32), pltpu.SemaphoreType.DMA((2,))],
        compiler_params=LIMIT,
    )(*operands)


def outer_call(*operands):
    return pl.pallas_call(
        outer_kernel,
        in_specs=[whole((4096, 128))] + [whole(EDGE)] * 4,
        out_specs=HBM,
        out_shape=jax.ShapeDtypeStruct((64, 8, 8, 128), BF16),
        scratch_shapes=[
            pltpu.VMEM((64, 8, 8, 128), BF16),
            pltpu.VMEM((1024, 128), F32),
            pltpu.SemaphoreType.DMA((2,)),
        ],
        compiler_params=LIMIT,
    )(*operands)


def tree_call(*operands):
    return pl.pallas_call(
        tree_kernel,
        in_specs=[SMEM, whole((63, 64, 128)), whole((64, 32, 128)), whole((64, 32, 128))],
        out_specs=HBM,
        out_shape=jax.ShapeDtypeStruct((64, 64, 127), F32),
        scratch_shapes=[
            pltpu.VMEM((63, 64, 128), BF16),
            pltpu.VMEM((128 * KEPT, 128), F32),
            pltpu.VMEM((64, 64, 127), F32),
            pltpu.SemaphoreType.DMA((4,)),
        ],
        compiler_params=LIMIT,
    )(*operands)


def local(states, class_map, perm_table, candidates, merge_order):
    tile = lax.axis_index("gx") * lax.axis_size("gy") + lax.axis_index("gy")
    where = tile.reshape(1).astype(jnp.int32)
    states, class_map, perm_table, candidates, merge_rows = (
        pltpu.with_memory_space_constraint(value, pltpu.HBM)
        for value in (states, class_map, perm_table, candidates.reshape(128, 64), merge_order)
    )
    states_shape = (2, 64, 8, 8, 128)
    low, high, to_minus, to_plus, own, cells, hits = edge_x_call(
        where, perm_table, class_map, candidates, merge_rows, states
    )

    def shift(value, axis, by):
        count = lax.axis_size(axis)
        return lax.ppermute(value, axis, [(i, (i + by) % count) for i in range(count)])

    from_minus = shift(to_plus, "gx", 1)
    from_plus = shift(to_minus, "gx", -1)

    side, perm, near_states = pl.pallas_call(
        edge_y_kernel,
        in_specs=[HBM, HBM, HBM],
        out_specs=[whole(SIDE), whole(CUBE), whole(states_shape)],
        out_shape=[
            jax.ShapeDtypeStruct(SIDE, BF16),
            jax.ShapeDtypeStruct(CUBE, F32),
            jax.ShapeDtypeStruct(states_shape, BF16),
        ],
        scratch_shapes=[pltpu.VMEM(CUBE, jnp.int32), pltpu.SMEM((8,), F32), pltpu.SemaphoreType.DMA((4,))],
        compiler_params=LIMIT,
    )(perm_table, class_map, states)
    side_low = shift(side, "gy", 1)
    side_high = shift(side, "gy", -1)

    inner = pl.pallas_call(
        inner_kernel,
        in_specs=[whole(CUBE), whole(states_shape)],
        out_specs=whole((4096, 128)),
        out_shape=jax.ShapeDtypeStruct((4096, 128), F32),
        scratch_shapes=FACES,
        compiler_params=LIMIT,
    )(perm, near_states)
    mine_rows, send_rows = middle_call(
        inner, cells, hits, side, side_low, side_high, own, from_minus, from_plus
    )

    swap = [(i, i ^ 1) for i in range(8)]
    got_rows = lax.ppermute(send_rows, "gy", swap)
    merged = mine_rows[:, :64] + got_rows[:, :64]
    top = merged.astype(BF16)
    rest = (merged - lax.reduce_precision(merged, 8, 7)).astype(BF16)
    spread = jnp.broadcast_to(jnp.concatenate([top, rest], 1)[None], (64, 32, 128))
    peers = [[i * 8 + j * 2 + c for i in range(16) for j in range(4)] for c in range(2)]
    spread, low, high, perm = lax.optimization_barrier((spread, low, high, perm))
    mine = lax.all_to_all(spread, ("gx", "gy"), 0, 0, axis_index_groups=peers)

    from_low = shift(high, "gx", 1)
    from_high = shift(low, "gx", -1)
    within = near_call(perm, side, side_low, side_high, states)
    flux = outer_call(within, low, high, from_low, from_high)
    numbers = lax.broadcasted_iota(jnp.int32, (63, 64, 128), 2)
    picks = (merge_order[64:, :64, None] == numbers).astype(BF16)
    mine, flux, picks = lax.optimization_barrier((mine, flux, picks))
    other = lax.ppermute(mine, "gy", swap)
    kept = tree_call(where, picks, mine, other)
    return flux, jnp.transpose(kept, (2, 0, 1))


def solution(mesh):
    in_specs = (P(None, None, None, "gx", "gy"), P(None, "gx", "gy"), P(), P(), P())
    out_specs = (P(None, None, "gx", "gy"), P())
    return jax.shard_map(local, mesh=mesh, in_specs=in_specs, out_specs=out_specs, check_vma=False)
```

```python
import jax
import jax.numpy as jnp
from jax import lax
from jax.experimental import pallas as pl
from jax.experimental.pallas import tpu as pltpu
from jax.sharding import PartitionSpec as P

F32 = jnp.float32
BF16 = jnp.bfloat16
KEPT = 72
CUBE = (8, 8, 128)
FLAT = (64, 128)
EDGE = (131, 8, 128)
SIDE = (5, 8, 8, 128)
HBM = pl.BlockSpec(memory_space=pltpu.HBM)
SMEM = pl.BlockSpec(memory_space=pltpu.SMEM)
LIMIT = pltpu.CompilerParams(vmem_limit_bytes=32 * 1024 * 1024)


def whole(shape):
    return pl.BlockSpec(shape, lambda *_: (0,) * len(shape))


def lane_of(shape):
    return lax.broadcasted_iota(jnp.int32, shape, len(shape) - 1)


def turn(value, by):
    return pltpu.roll(value, by, 1)


def look_up(kind, table_ref):
    value = jnp.zeros(kind.shape, F32)
    for number in range(8):
        value = jnp.where(kind == number, table_ref[number], value)
    return value


def trans(k_here, k_next):
    return k_here * k_next / (k_here + k_next)


def face(t, m_here, m_next, p_here, p_next):
    return t * (m_here + m_next) * (p_next - p_here)


def three_pieces(value):
    high = value.astype(BF16)
    rest = value - high.astype(F32)
    middle = rest.astype(BF16)
    return high, middle, (rest - middle.astype(F32)).astype(BF16)


def two_times(weights):
    return jnp.concatenate([weights, weights], 0)


def two_pieces(value):
    high = value.astype(BF16)
    return jnp.concatenate([high, (value - high.astype(F32)).astype(BF16)], 1)


def matmul(left, right):
    return jnp.dot(left, right, preferred_element_type=F32)


def sub_of(shape):
    return lax.broadcasted_iota(jnp.int32, shape, 0)


def slots_of(order_row, cand_row, core):
    lane = lane_of(FLAT)
    order = jnp.broadcast_to(order_row, FLAT)
    swapped = jnp.where(lane < 32, turn(order, 96), turn(order, 32))
    order = jnp.where(core == 1, swapped, order)
    match = (order == core * 64 + sub_of(FLAT)) & (lane < 64)
    column = jnp.transpose(jnp.broadcast_to(cand_row.astype(F32), (64, 64)))[:, :1]
    cell = jnp.sum(jnp.where(match, jnp.broadcast_to(column, FLAT) + 1.0, 0.0), 0, keepdims=True)
    cell = cell.astype(jnp.int32) - 1
    return jnp.where(cell < 0, -1, cell % 128), jnp.where(cell < 0, -1, cell // 128)


def one_hot(shape, at):
    return jnp.where(sub_of(shape) == at, 1.0, 0.0)


def edge_kernel(
    where_ref, table_hbm, class_hbm, cand_hbm, order_hbm, states_hbm,
    low_ref, high_ref, to_minus_ref, to_plus_ref, own_ref, cells_ref, hits_ref, side_ref, perm_ref, states_ref,
    class_ref, cand_ref, order_ref, table_ref, wide_ref, weights_ref, product_ref, sem,
):
    tile = where_ref[0]
    core = tile % 2
    tiles = (tile, (tile + 120) % 128, (tile + 8) % 128)
    copies = [
        pltpu.make_async_copy(table_hbm, table_ref, sem.at[0]),
        pltpu.make_async_copy(class_hbm, class_ref, sem.at[1]),
    ]
    for n, at in enumerate(tiles):
        copies.append(pltpu.make_async_copy(cand_hbm.at[pl.ds(at, 1)], cand_ref.at[n], sem.at[2 + n]))
        copies.append(pltpu.make_async_copy(order_hbm.at[pl.ds(at // 2, 1)], order_ref.at[n], sem.at[5 + n]))
    for n in range(2):
        half = pl.ds(32 * n, 32)
        copies.append(pltpu.make_async_copy(states_hbm.at[:, half], states_ref.at[:, half], sem.at[8 + n]))
    for copy in copies:
        copy.start()
    for copy in copies[:8]:
        copy.wait()
    perm = look_up(class_ref[...], table_ref)
    perm_ref[...] = perm
    first = jnp.broadcast_to(perm[:, :, 0:1], CUBE)
    last = jnp.broadcast_to(perm[:, :, 127:128], CUBE)
    for n, piece in enumerate(three_pieces(jnp.where(lane_of(CUBE) % 2 == 0, first, last))):
        side_ref[2 + n] = piece
    wide_ref[pl.ds(0, 64), :] = perm.reshape(FLAT)
    for ref, at in ((low_ref, 0), (high_ref, 7)):
        for n, piece in enumerate(three_pieces(wide_ref[pl.ds(at, 8, stride=8), :])):
            ref[128 + n] = piece
    own_y, own_zx = slots_of(order_ref[0], cand_ref[0], core)
    minus_y, minus_zx = slots_of(order_ref[1], cand_ref[1], core)
    plus_y, plus_zx = slots_of(order_ref[2], cand_ref[2], core)
    square, rows_of_z = (128, 128), (8, 128)
    own_cells = one_hot(square, own_y).astype(BF16)
    cells_ref[...] = two_times(own_cells)
    hits_ref[...] = one_hot(FLAT, own_zx)
    weights_ref[0] = jnp.concatenate([one_hot(square, minus_y).astype(BF16), own_cells], 1)
    weights_ref[1] = jnp.concatenate([one_hot(square, plus_y).astype(BF16), own_cells], 1)
    own_z = sub_of(rows_of_z) * 8
    mask_low = jnp.concatenate(
        [one_hot(rows_of_z, jnp.where(minus_zx < 0, -1, minus_zx // 8)), jnp.where(own_z == own_zx, 1.0, 0.0)], 1
    )
    mask_high = jnp.concatenate(
        [one_hot(rows_of_z, jnp.where(plus_zx < 0, -1, plus_zx // 8)), jnp.where(own_z + 7 == own_zx, 1.0, 0.0)], 1
    )
    at_low = jnp.where((own_zx >= 0) & (own_zx % 8 == 0), 1.0, 0.0)
    at_high = jnp.where((own_zx >= 0) & (own_zx % 8 == 7), 1.0, 0.0)
    flag = sub_of(rows_of_z)
    flags = jnp.where(flag == 0, at_low, jnp.where(flag == 1, at_high, 0.0))
    lane = lane_of(FLAT)
    acc = [jnp.zeros(FLAT, F32), jnp.zeros(FLAT, F32)]
    for snap in range(64):
        if snap % 32 == 0:
            copies[8 + snap // 32].wait()
        keep = (lane == 2 * snap) | (lane == (2 * snap + 127) % 128)
        for field in range(2):
            slot = (1 + field + 2 * snap) * 64
            value = states_ref[field, snap].astype(F32).reshape(FLAT)
            acc[field] = jnp.where(keep, turn(value, 2 * snap), acc[field])
            wide_ref[pl.ds(slot, 64), :] = value
            low_ref[field * 64 + snap] = wide_ref[pl.ds(slot, 8, stride=8), :].astype(BF16)
            high_ref[field * 64 + snap] = wide_ref[pl.ds(slot + 7, 8, stride=8), :].astype(BF16)

    for field in range(2):
        side_ref[field] = acc[field].reshape(CUBE).astype(BF16)

    def select(ref, weights, mask):
        for first, count in [(16 * n, 16) for n in range(8)] + [(128, 3)]:
            rows = matmul(ref[pl.ds(first, count)].reshape(count * 8, 128), weights)
            for n in range(count):
                product = rows[n * 8 : n * 8 + 8] * mask
                for half in range(2):
                    product_ref[half, pl.ds((first + n) * 8, 8), :] = product[:, half * 128 : half * 128 + 128]
        halves = []
        for half in range(2):
            product_ref[half, pl.ds(131 * 8, 40), :] = jnp.zeros((40, 128), F32)
            total = product_ref[half, pl.ds(0, 136, stride=8), :]
            for z in range(1, 8):
                total = total + product_ref[half, pl.ds(z, 136, stride=8), :]
            halves.append(total)
        return halves

    def pack(rows):
        return jnp.concatenate([rows[:64] + turn(rows[64:128], 64), rows[128:136]], 0).astype(BF16)

    to_minus, own_low = select(low_ref, weights_ref[0], mask_low)
    to_plus, own_high = select(high_ref, weights_ref[1], mask_high)
    to_minus_ref[...] = pack(to_minus)
    to_plus_ref[...] = pack(to_plus)
    own_ref[pl.ds(0, 136), :] = own_low + own_high
    own_ref[pl.ds(136, 8), :] = flags


def set_up_faces(perm, tx_ref, ty_ref, tz_ref, shift_ref):
    row = lax.broadcasted_iota(jnp.int32, CUBE, 1)
    next_y = turn(perm.reshape(FLAT), 127).reshape(CUBE)
    tx_ref[...] = jnp.where(row == 7, 0.0, trans(perm, jnp.roll(perm, -1, 1)))
    ty_ref[...] = jnp.where(lane_of(CUBE) == 127, 0.0, trans(perm, next_y)).reshape(FLAT)
    tz_ref[...] = trans(perm[:-1], perm[1:])
    square = (128, 128)
    shift_ref[...] = jnp.where(sub_of(square) == lane_of(square) + 1, 1.0, 0.0).astype(BF16)


def flux_within(states_ref, snap, tx_ref, ty_ref, tz_ref, shift_ref):
    p = states_ref[0, snap].astype(F32)
    s = states_ref[1, snap].astype(F32)
    m = s * s
    fx = face(tx_ref[...], m, jnp.roll(m, -1, 1), p, jnp.roll(p, -1, 1))
    total = fx - jnp.roll(fx, 1, 1)
    p_next = matmul(states_ref[0, snap].reshape(FLAT), shift_ref[...])
    s_next = matmul(states_ref[1, snap].reshape(FLAT), shift_ref[...])
    fy = face(ty_ref[...], m.reshape(FLAT), s_next * s_next, p.reshape(FLAT), p_next)
    total = total + (fy - turn(fy, 1)).reshape(CUBE)
    fz = face(tz_ref[...], m[:-1], m[1:], p[:-1], p[1:])
    zero = jnp.zeros((1, 8, 128), F32)
    total = total + (jnp.concatenate([fz, zero], 0) - jnp.concatenate([zero, fz], 0))
    return total.reshape(FLAT)


def inner_kernel(perm_ref, states_ref, out_ref, tx_ref, ty_ref, tz_ref, shift_ref):
    faces = (tx_ref, ty_ref, tz_ref, shift_ref)
    set_up_faces(perm_ref[...], *faces)

    def group(number, carry):
        for k in range(16):
            snap = number * 16 + k
            span = pl.ds(pl.multiple_of(snap * 64, 64), 64)
            out_ref[span, :] = flux_within(states_ref, snap, *faces)
        return carry

    lax.fori_loop(0, 4, group, 0)


def sum_of_eights(picked_ref):
    total = picked_ref[pl.ds(0, 64, stride=8), :]
    for at in range(1, 8):
        total = total + picked_ref[pl.ds(at, 64, stride=8), :]
    return total


def perm_of(ref, at):
    high, middle, low = (ref[at + n].astype(F32) for n in range(3))
    return (high + middle) + low


def flux_across_y(side_ref, side_low_ref, side_high_ref):
    lane = lane_of(FLAT)

    def beyond(below, above):
        below, above = below.reshape(FLAT), above.reshape(FLAT)
        return jnp.where(lane % 2 == 0, turn(below, 1), turn(above, 127))

    t_side = trans(
        perm_of(side_ref, 2).reshape(FLAT), beyond(perm_of(side_low_ref, 2), perm_of(side_high_ref, 2))
    )

    def side_pair(which):
        here = side_ref[which].astype(F32).reshape(FLAT)
        return here, beyond(side_low_ref[which].astype(F32), side_high_ref[which].astype(F32))

    p_here, p_next = side_pair(0)
    s_here, s_next = side_pair(1)
    return face(t_side, s_here * s_here, s_next * s_next, p_here, p_next)


def sides_of(qy_ref, snap):
    lane = lane_of(FLAT)
    turned = turn(qy_ref[...], (128 - 2 * snap) % 128)
    return jnp.where((lane == 0) | (lane == 127), turned, 0.0)


def middle_kernel(
    inner_ref, cells_ref, hits_ref, side_ref, side_low_ref, side_high_ref, own_ref, from_minus_ref, from_plus_ref,
    mine_ref, send_ref, qy_ref, picked_ref,
):
    qy_ref[...] = flux_across_y(side_ref, side_low_ref, side_high_ref)
    for snap in range(64):
        flux = inner_ref[pl.ds(snap * 64, 64), :] + sides_of(qy_ref, snap)
        rows = matmul(two_pieces(flux), cells_ref[...]) * hits_ref[...]
        picked_ref[pl.ds(snap * 8, 8), :] = jnp.sum(rows.reshape(CUBE), 0)
    at_low, at_high = own_ref[pl.ds(136, 1), :], own_ref[pl.ds(137, 1), :]
    beside = from_minus_ref[...].astype(F32) * at_low + from_plus_ref[...].astype(F32) * at_high
    sat = from_minus_ref[:64].astype(F32) * turn(at_low, 64) + from_plus_ref[:64].astype(F32) * turn(at_high, 64)
    m_next, p_next = turn(sat, 64), beside[:64]
    p_own, m_own = own_ref[pl.ds(0, 64), :], own_ref[pl.ds(64, 64), :]
    k_next = (beside[64:65] + beside[65:66]) + beside[66:67]
    k_own = (own_ref[pl.ds(128, 1), :] + own_ref[pl.ds(129, 1), :]) + own_ref[pl.ds(130, 1), :]
    k_sum = jnp.where(at_low + at_high > 0.0, k_own + k_next, 1.0)
    q_x = face(k_own * k_next / k_sum, m_own * m_own, m_next * m_next, p_own, p_next)
    total = sum_of_eights(picked_ref) + q_x
    rows = jnp.transpose(jnp.concatenate([total, jnp.zeros(FLAT, F32)], 0))
    mine_ref[...] = rows[:32]
    send_ref[...] = rows[32:64]


def near_kernel(
    perm_ref, side_ref, side_low_ref, side_high_ref, states_hbm, out_ref,
    states_ref, tx_ref, ty_ref, tz_ref, shift_ref, qy_ref, sem,
):
    copies = []
    for n in range(2):
        half = pl.ds(32 * n, 32)
        copies.append(pltpu.make_async_copy(states_hbm.at[:, half], states_ref.at[:, half], sem.at[n]))
        copies[n].start()
    faces = (tx_ref, ty_ref, tz_ref, shift_ref)
    set_up_faces(perm_ref[...], *faces)
    qy_ref[...] = flux_across_y(side_ref, side_low_ref, side_high_ref)

    def group(number, carry):
        for k in range(16):
            snap = number * 16 + k
            span = pl.ds(pl.multiple_of(snap * 64, 64), 64)
            out_ref[span, :] = flux_within(states_ref, snap, *faces) + sides_of(qy_ref, snap)
        return carry

    for n in range(2):
        copies[n].wait()
        lax.fori_loop(2 * n, 2 * n + 2, group, 0)


def outer_kernel(within_ref, low_ref, high_ref, from_low_ref, from_high_ref, out_hbm, out_ref, edge_ref, sem):
    t_low = trans(perm_of(low_ref, 128), perm_of(from_low_ref, 128))
    t_high = trans(perm_of(high_ref, 128), perm_of(from_high_ref, 128))
    edge_ref[...] = jnp.zeros_like(edge_ref)

    def edge(own_ref, other_ref, t, snap):
        s_here, s_next = own_ref[64 + snap].astype(F32), other_ref[64 + snap].astype(F32)
        p_here, p_next = own_ref[snap].astype(F32), other_ref[snap].astype(F32)
        return face(t, s_here * s_here, s_next * s_next, p_here, p_next)

    def put(part):
        span = pl.ds(part * 32, 32)
        return pltpu.make_async_copy(out_ref.at[span], out_hbm.at[span], sem.at[part])

    def group(number, carry):
        for k in range(16):
            snap = number * 16 + k
            edge_ref[pl.ds(k * 64, 8, stride=8), :] = edge(low_ref, from_low_ref, t_low, snap)
            edge_ref[pl.ds(k * 64 + 7, 8, stride=8), :] = edge(high_ref, from_high_ref, t_high, snap)
        for k in range(16):
            snap = number * 16 + k
            flux = within_ref[pl.ds(pl.multiple_of(snap * 64, 64), 64), :] + edge_ref[pl.ds(k * 64, 64), :]
            out_ref[snap] = flux.reshape(CUBE).astype(BF16)
        return carry

    for part in range(2):
        lax.fori_loop(2 * part, 2 * part + 2, group, 0)
        put(part).start()
    for part in range(2):
        put(part).wait()


def tree_kernel(where_ref, pick_ref, mine_ref, other_ref, out_hbm, level_ref, kept_ref, out_ref, sem):
    def select(node, stack):
        got = matmul(pick_ref[node - 64], stack)
        kept_ref[pl.ds(node * KEPT, 64), :] = got
        level_ref[node - 64] = got.astype(BF16)

    def first_levels(low_ref, high_ref):
        for j in range(32):
            pair = [low_ref[2 * j], high_ref[2 * j], low_ref[2 * j + 1], high_ref[2 * j + 1]]
            select(64 + j, jnp.concatenate(pair, 0))
        for chip in range(64):
            kept_ref[pl.ds(chip * KEPT, 32), :] = low_ref[chip].astype(F32)
            kept_ref[pl.ds(chip * KEPT + 32, 32), :] = high_ref[chip].astype(F32)

    @pl.when(where_ref[0] % 2 == 0)
    def _():
        first_levels(mine_ref, other_ref)

    @pl.when(where_ref[0] % 2 == 1)
    def _():
        first_levels(other_ref, mine_ref)

    before, offset, count = 64, 96, 16
    while count >= 1:
        for j in range(count):
            select(offset + j, level_ref[pl.ds(before + 2 * j - 64, 2)].reshape(128, 128))
        before, offset, count = offset, offset + count, count // 2

    def put(at):
        span = pl.ds(at, 16)
        return pltpu.make_async_copy(out_ref.at[span], out_hbm.at[span], sem.at[at // 16])

    for slot in range(64):
        turned = jnp.transpose(kept_ref[pl.ds(slot, 128, stride=KEPT), :])
        out_ref[slot] = (turned[:64] + turned[64:])[:, :127]
        if slot % 16 == 15:
            put(slot - 15).start()
    for at in range(0, 64, 16):
        put(at).wait()


ROWS = jax.ShapeDtypeStruct((32, 128), F32)
SLOTS = (72, 128)
OWN = (144, 128)


def edge_call(*operands):
    edge, slots = jax.ShapeDtypeStruct(EDGE, BF16), jax.ShapeDtypeStruct(SLOTS, BF16)
    shapes = [
        edge, edge, slots, slots, jax.ShapeDtypeStruct(OWN, F32),
        jax.ShapeDtypeStruct((256, 128), BF16), jax.ShapeDtypeStruct(FLAT, F32),
        jax.ShapeDtypeStruct(SIDE, BF16), jax.ShapeDtypeStruct(CUBE, F32),
        jax.ShapeDtypeStruct((2, 64, 8, 8, 128), BF16),
    ]
    return pl.pallas_call(
        edge_kernel,
        in_specs=[SMEM] + [HBM] * 5,
        out_specs=[whole(one.shape) for one in shapes],
        out_shape=shapes,
        scratch_shapes=[
            pltpu.VMEM(CUBE, jnp.int32),
            pltpu.VMEM((3, 1, 64), jnp.int32),
            pltpu.VMEM((3, 1, 128), jnp.int32),
            pltpu.SMEM((8,), F32),
            pltpu.VMEM((129 * 64, 128), F32),
            pltpu.VMEM((2, 128, 256), BF16),
            pltpu.VMEM((2, 136 * 8, 128), F32),
            pltpu.SemaphoreType.DMA((10,)),
        ],
        compiler_params=LIMIT,
    )(*operands)


def middle_call(*operands):
    return pl.pallas_call(
        middle_kernel,
        in_specs=[whole((4096, 128)), whole((256, 128)), whole(FLAT)]
        + [whole(SIDE)] * 3 + [whole(OWN), whole(SLOTS), whole(SLOTS)],
        out_specs=[whole((32, 128)), whole((32, 128))],
        out_shape=[ROWS, ROWS],
        scratch_shapes=[pltpu.VMEM(FLAT, F32), pltpu.VMEM((512, 128), F32)],
        compiler_params=LIMIT,
    )(*operands)


FACES = [
    pltpu.VMEM(CUBE, F32), pltpu.VMEM(FLAT, F32), pltpu.VMEM((7, 8, 128), F32), pltpu.VMEM((128, 128), BF16)
]


def near_call(*operands):
    return pl.pallas_call(
        near_kernel,
        in_specs=[whole(CUBE)] + [whole(SIDE)] * 3 + [HBM],
        out_specs=whole((4096, 128)),
        out_shape=jax.ShapeDtypeStruct((4096, 128), F32),
        scratch_shapes=[pltpu.VMEM((2, 64, 8, 8, 128), BF16)]
        + FACES
        + [pltpu.VMEM(FLAT, F32), pltpu.SemaphoreType.DMA((2,))],
        compiler_params=LIMIT,
    )(*operands)


def outer_call(*operands):
    return pl.pallas_call(
        outer_kernel,
        in_specs=[whole((4096, 128))] + [whole(EDGE)] * 4,
        out_specs=HBM,
        out_shape=jax.ShapeDtypeStruct((64, 8, 8, 128), BF16),
        scratch_shapes=[
            pltpu.VMEM((64, 8, 8, 128), BF16),
            pltpu.VMEM((1024, 128), F32),
            pltpu.SemaphoreType.DMA((2,)),
        ],
        compiler_params=LIMIT,
    )(*operands)


def tree_call(*operands):
    return pl.pallas_call(
        tree_kernel,
        in_specs=[SMEM, whole((63, 64, 128)), whole((64, 32, 128)), whole((64, 32, 128))],
        out_specs=HBM,
        out_shape=jax.ShapeDtypeStruct((64, 64, 127), F32),
        scratch_shapes=[
            pltpu.VMEM((63, 64, 128), BF16),
            pltpu.VMEM((128 * KEPT, 128), F32),
            pltpu.VMEM((64, 64, 127), F32),
            pltpu.SemaphoreType.DMA((4,)),
        ],
        compiler_params=LIMIT,
    )(*operands)


def local(states, class_map, perm_table, candidates, merge_order):
    tile = lax.axis_index("gx") * lax.axis_size("gy") + lax.axis_index("gy")
    where = tile.reshape(1).astype(jnp.int32)
    states, class_map, perm_table, candidates, merge_rows = (
        pltpu.with_memory_space_constraint(value, pltpu.HBM)
        for value in (states, class_map, perm_table, candidates.reshape(128, 64), merge_order)
    )
    low, high, to_minus, to_plus, own, cells, hits, side, perm, near_states = edge_call(
        where, perm_table, class_map, candidates, merge_rows, states
    )

    def shift(value, axis, by):
        count = lax.axis_size(axis)
        return lax.ppermute(value, axis, [(i, (i + by) % count) for i in range(count)])

    from_minus = shift(to_plus, "gx", 1)
    from_plus = shift(to_minus, "gx", -1)

    side_low = shift(side, "gy", 1)
    side_high = shift(side, "gy", -1)

    inner = pl.pallas_call(
        inner_kernel,
        in_specs=[whole(CUBE), whole((2, 64, 8, 8, 128))],
        out_specs=whole((4096, 128)),
        out_shape=jax.ShapeDtypeStruct((4096, 128), F32),
        scratch_shapes=FACES,
        compiler_params=LIMIT,
    )(perm, near_states)
    mine_rows, send_rows = middle_call(
        inner, cells, hits, side, side_low, side_high, own, from_minus, from_plus
    )

    swap = [(i, i ^ 1) for i in range(8)]
    got_rows = lax.ppermute(send_rows, "gy", swap)
    merged = mine_rows[:, :64] + got_rows[:, :64]
    top = merged.astype(BF16)
    rest = (merged - lax.reduce_precision(merged, 8, 7)).astype(BF16)
    spread = jnp.broadcast_to(jnp.concatenate([top, rest], 1)[None], (64, 32, 128))
    peers = [[i * 8 + j * 2 + c for i in range(16) for j in range(4)] for c in range(2)]
    spread, perm = lax.optimization_barrier((spread, perm))
    mine = lax.all_to_all(spread, ("gx", "gy"), 0, 0, axis_index_groups=peers)

    from_low = shift(high, "gx", 1)
    from_high = shift(low, "gx", -1)
    within = near_call(perm, side, side_low, side_high, states)
    flux = outer_call(within, low, high, from_low, from_high)
    flux, orders = lax.optimization_barrier((flux, merge_order))
    numbers = lax.broadcasted_iota(jnp.int32, (63, 64, 128), 2)
    picks = (orders[64:, :64, None] == numbers).astype(BF16)
    mine, flux, picks = lax.optimization_barrier((mine, flux, picks))
    other = lax.ppermute(mine, "gy", swap)
    kept = tree_call(where, picks, mine, other)
    return flux, jnp.transpose(kept, (2, 0, 1))


def solution(mesh):
    in_specs = (P(None, None, None, "gx", "gy"), P(None, "gx", "gy"), P(), P(), P())
    out_specs = (P(None, None, "gx", "gy"), P())
    return jax.shard_map(local, mesh=mesh, in_specs=in_specs, out_specs=out_specs, check_vma=False)
```

```python
import jax
import jax.numpy as jnp
from jax import lax
from jax.experimental import pallas as pl
from jax.experimental.pallas import tpu as pltpu
from jax.sharding import PartitionSpec as P

F32 = jnp.float32
BF16 = jnp.bfloat16
KEPT = 72
UNROLL = 64
CUBE = (8, 8, 128)
FLAT = (64, 128)
EDGE = (131, 8, 128)
SIDE = (5, 8, 8, 128)
HBM = pl.BlockSpec(memory_space=pltpu.HBM)
SMEM = pl.BlockSpec(memory_space=pltpu.SMEM)
LIMIT = pltpu.CompilerParams(vmem_limit_bytes=48 * 1024 * 1024)


def whole(shape):
    return pl.BlockSpec(shape, lambda *_: (0,) * len(shape))


def lane_of(shape):
    return lax.broadcasted_iota(jnp.int32, shape, len(shape) - 1)


def turn(value, by):
    return pltpu.roll(value, by, 1)


def look_up(kind, table_ref):
    value = jnp.zeros(kind.shape, F32)
    for number in range(8):
        value = jnp.where(kind == number, table_ref[number], value)
    return value


def trans(k_here, k_next):
    return k_here * k_next / (k_here + k_next)


def face(t, m_here, m_next, p_here, p_next):
    return t * (m_here + m_next) * (p_next - p_here)


def three_pieces(value):
    high = value.astype(BF16)
    rest = value - high.astype(F32)
    middle = rest.astype(BF16)
    return high, middle, (rest - middle.astype(F32)).astype(BF16)


def edge_x_kernel(
    table_hbm, class_hbm, states_hbm, low_ref, high_ref, states_ref, class_ref, table_ref, wide_ref, sem
):
    copies = [
        pltpu.make_async_copy(table_hbm, table_ref, sem.at[0]),
        pltpu.make_async_copy(class_hbm, class_ref, sem.at[1]),
    ]
    for n, rows in enumerate((pl.ds(0, 2), pl.ds(6, 2))):
        copies.append(
            pltpu.make_async_copy(states_hbm.at[:, :, :, rows], states_ref.at[:, :, :, rows], sem.at[2 + n])
        )
    for copy in copies:
        copy.start()
    copies[0].wait()
    copies[1].wait()
    wide_ref[pl.ds(0, 64), :] = look_up(class_ref[...], table_ref).reshape(FLAT)
    for ref, at in ((low_ref, 0), (high_ref, 7)):
        for n, piece in enumerate(three_pieces(wide_ref[pl.ds(at, 8, stride=8), :])):
            ref[128 + n] = piece
    copies[2].wait()
    copies[3].wait()
    for snap in range(64):
        for field in range(2):
            slot = (1 + field + 2 * snap) * 64
            wide_ref[pl.ds(slot, 64), :] = states_ref[field, snap].astype(F32).reshape(FLAT)
            low_ref[field * 64 + snap] = wide_ref[pl.ds(slot, 8, stride=8), :].astype(BF16)
            high_ref[field * 64 + snap] = wide_ref[pl.ds(slot + 7, 8, stride=8), :].astype(BF16)


def two_times(weights):
    return jnp.concatenate([weights, weights], 0)


def two_pieces(value):
    high = value.astype(BF16)
    return jnp.concatenate([high, (value - high.astype(F32)).astype(BF16)], 1)


def matmul(left, right):
    return jnp.dot(left, right, preferred_element_type=F32)


def sub_of(shape):
    return lax.broadcasted_iota(jnp.int32, shape, 0)


def edge_y_kernel(
    where_ref, table_hbm, class_hbm, cand_hbm, order_hbm, states_hbm,
    side_ref, perm_ref, states_ref, cells_ref, hits_ref, class_ref, cand_ref, order_ref, table_ref, sem,
):
    tile = where_ref[0]
    core = tile % 2
    copies = [
        pltpu.make_async_copy(table_hbm, table_ref, sem.at[0]),
        pltpu.make_async_copy(class_hbm, class_ref, sem.at[1]),
        pltpu.make_async_copy(cand_hbm.at[pl.ds(tile, 1)], cand_ref, sem.at[2]),
        pltpu.make_async_copy(order_hbm.at[pl.ds(tile // 2, 1)], order_ref, sem.at[3]),
    ]
    for n in range(2):
        half = pl.ds(32 * n, 32)
        copies.append(pltpu.make_async_copy(states_hbm.at[:, half], states_ref.at[:, half], sem.at[4 + n]))
    for copy in copies:
        copy.start()
    for copy in copies[:4]:
        copy.wait()
    lane = lane_of(FLAT)
    order = jnp.broadcast_to(order_ref[...], FLAT)
    swapped = jnp.where(lane < 32, turn(order, 96), turn(order, 32))
    order = jnp.where(core == 1, swapped, order)
    match = (order == core * 64 + sub_of(FLAT)) & (lane < 64)
    column = jnp.transpose(jnp.broadcast_to(cand_ref[...].astype(F32), (64, 64)))[:, :1]
    cell = jnp.sum(jnp.where(match, jnp.broadcast_to(column, FLAT) + 1.0, 0.0), 0, keepdims=True)
    cell = cell.astype(jnp.int32) - 1
    at_y = jnp.where(cell < 0, -1, cell % 128)
    at_zx = jnp.where(cell < 0, -1, cell // 128)
    cells_ref[...] = two_times(jnp.where(sub_of((128, 128)) == at_y, 1.0, 0.0).astype(BF16))
    hits_ref[...] = jnp.where(sub_of(FLAT) == at_zx, 1.0, 0.0)

    perm = look_up(class_ref[...], table_ref)
    perm_ref[...] = perm
    first = jnp.broadcast_to(perm[:, :, 0:1], CUBE)
    last = jnp.broadcast_to(perm[:, :, 127:128], CUBE)
    for n, piece in enumerate(three_pieces(jnp.where(lane_of(CUBE) % 2 == 0, first, last))):
        side_ref[2 + n] = piece
    square = (128, 128)
    spread = jnp.where(sub_of(square) == jnp.where(lane_of(square) % 2 == 0, 0, 127), 1.0, 0.0).astype(BF16)
    acc = [jnp.zeros(FLAT, F32), jnp.zeros(FLAT, F32)]
    for snap in range(64):
        if snap % 32 == 0:
            copies[4 + snap // 32].wait()
        keep = (lane == 2 * snap) | (lane == (2 * snap + 127) % 128)
        for field in range(2):
            value = matmul(states_ref[field, snap].reshape(FLAT), spread)
            acc[field] = jnp.where(keep, value, acc[field])
    for field in range(2):
        side_ref[field] = acc[field].reshape(CUBE).astype(BF16)


def inner_kernel(perm_ref, states_ref, out_ref, tx_ref, ty_ref, tz_ref, shift_ref):
    perm = perm_ref[...]
    row = lax.broadcasted_iota(jnp.int32, CUBE, 1)
    next_y = turn(perm.reshape(FLAT), 127).reshape(CUBE)
    tx_ref[...] = jnp.where(row == 7, 0.0, trans(perm, jnp.roll(perm, -1, 1)))
    ty_ref[...] = jnp.where(lane_of(CUBE) == 127, 0.0, trans(perm, next_y)).reshape(FLAT)
    tz_ref[...] = trans(perm[:-1], perm[1:])
    square = (128, 128)
    shift_ref[...] = jnp.where(sub_of(square) == lane_of(square) + 1, 1.0, 0.0).astype(BF16)

    def group(number, carry):
        for k in range(16):
            snap = number * 16 + k
            p = states_ref[0, snap].astype(F32)
            s = states_ref[1, snap].astype(F32)
            m = s * s
            fx = face(tx_ref[...], m, jnp.roll(m, -1, 1), p, jnp.roll(p, -1, 1))
            total = fx - jnp.roll(fx, 1, 1)
            p_next = matmul(states_ref[0, snap].reshape(FLAT), shift_ref[...])
            s_next = matmul(states_ref[1, snap].reshape(FLAT), shift_ref[...])
            fy = face(ty_ref[...], m.reshape(FLAT), s_next * s_next, p.reshape(FLAT), p_next)
            total = total + (fy - turn(fy, 1)).reshape(CUBE)
            fz = face(tz_ref[...], m[:-1], m[1:], p[:-1], p[1:])
            zero = jnp.zeros((1, 8, 128), F32)
            total = total + (jnp.concatenate([fz, zero], 0) - jnp.concatenate([zero, fz], 0))
            out_ref[pl.ds(pl.multiple_of(snap * 64, 64), 64), :] = total.reshape(FLAT)
        return carry

    lax.fori_loop(0, 4, group, 0)


def sum_of_eights(picked_ref):
    total = picked_ref[pl.ds(0, 64, stride=8), :]
    for at in range(1, 8):
        total = total + picked_ref[pl.ds(at, 64, stride=8), :]
    return total


def perm_of(ref, at):
    high, middle, low = (ref[at + n].astype(F32) for n in range(3))
    return (high + middle) + low


def middle_kernel(
    inner_ref, cells_ref, hits_ref, side_ref, side_low_ref, side_high_ref, flux_ref, rows_ref, qy_ref, picked_ref
):
    lane = lane_of(FLAT)

    def beyond(below, above):
        below, above = below.reshape(FLAT), above.reshape(FLAT)
        return jnp.where(lane % 2 == 0, turn(below, 1), turn(above, 127))

    t_side = trans(
        perm_of(side_ref, 2).reshape(FLAT), beyond(perm_of(side_low_ref, 2), perm_of(side_high_ref, 2))
    )

    def side_pair(which):
        here = side_ref[which].astype(F32).reshape(FLAT)
        return here, beyond(side_low_ref[which].astype(F32), side_high_ref[which].astype(F32))

    p_here, p_next = side_pair(0)
    s_here, s_next = side_pair(1)
    qy_ref[...] = face(t_side, s_here * s_here, s_next * s_next, p_here, p_next)
    at_edge = (lane == 0) | (lane == 127)

    def group(number, carry):
        for k in range(UNROLL):
            snap = number * UNROLL + k
            span = pl.ds(pl.multiple_of(snap * 64, 64), 64)
            turned = turn(qy_ref[...], (128 - 2 * snap) % 128)
            flux = inner_ref[span, :] + jnp.where(at_edge, turned, 0.0)
            flux_ref[span, :] = flux
            rows = matmul(two_pieces(flux), cells_ref[...]) * hits_ref[...]
            picked_ref[pl.ds(pl.multiple_of(snap * 8, 8), 8), :] = jnp.sum(rows.reshape(CUBE), 0)
        return carry

    lax.fori_loop(0, 64 // UNROLL, group, 0)
    rows_ref[...] = sum_of_eights(picked_ref)


def outer_rows_kernel(
    rows_ref, cells_ref, hits_ref, low_ref, high_ref, from_low_ref, from_high_ref,
    mine_ref, send_ref, qx_ref, picked_ref,
):
    t_low = trans(perm_of(low_ref, 128), perm_of(from_low_ref, 128))
    t_high = trans(perm_of(high_ref, 128), perm_of(from_high_ref, 128))

    def edge(own_ref, other_ref, t, snap):
        s_here, s_next = own_ref[64 + snap].astype(F32), other_ref[64 + snap].astype(F32)
        p_here, p_next = own_ref[snap].astype(F32), other_ref[snap].astype(F32)
        return face(t, s_here * s_here, s_next * s_next, p_here, p_next)

    for snap in range(64):
        qx_ref[pl.ds(snap * 16, 8), :] = edge(low_ref, from_low_ref, t_low, snap)
        qx_ref[pl.ds(snap * 16 + 8, 8), :] = edge(high_ref, from_high_ref, t_high, snap)
    hit_low, hit_high = hits_ref[pl.ds(0, 8, stride=8), :], hits_ref[pl.ds(7, 8, stride=8), :]
    for part in range(4):
        rows = matmul(two_pieces(qx_ref[pl.ds(part * 256, 256), :]), cells_ref[...])
        for k in range(16):
            low = rows[k * 16 : k * 16 + 8] * hit_low
            high = rows[k * 16 + 8 : k * 16 + 16] * hit_high
            picked_ref[pl.ds((part * 16 + k) * 8, 8), :] = low + high
    total = rows_ref[...] + sum_of_eights(picked_ref)
    rows = jnp.transpose(jnp.concatenate([total, jnp.zeros(FLAT, F32)], 0))
    mine_ref[...] = rows[:32]
    send_ref[...] = rows[32:64]


def outer_flux_kernel(within_ref, qx_ref, out_hbm, out_ref, edge_ref, sem):
    edge_ref[...] = jnp.zeros_like(edge_ref)

    def put(part):
        span = pl.ds(part * 32, 32)
        return pltpu.make_async_copy(out_ref.at[span], out_hbm.at[span], sem.at[part])

    def group(number, carry):
        for k in range(16):
            at = pl.multiple_of((number * 16 + k) * 16, 16)
            edge_ref[pl.ds(k * 64, 8, stride=8), :] = qx_ref[pl.ds(at, 8), :]
            edge_ref[pl.ds(k * 64 + 7, 8, stride=8), :] = qx_ref[pl.ds(at + 8, 8), :]
        for k in range(16):
            snap = number * 16 + k
            flux = within_ref[pl.ds(pl.multiple_of(snap * 64, 64), 64), :] + edge_ref[pl.ds(k * 64, 64), :]
            out_ref[snap] = flux.reshape(CUBE).astype(BF16)
        return carry

    for part in range(2):
        lax.fori_loop(2 * part, 2 * part + 2, group, 0)
        put(part).start()
    for part in range(2):
        put(part).wait()


def tree_kernel(where_ref, pick_ref, mine_ref, other_ref, out_hbm, level_ref, kept_ref, out_ref, sem):
    def select(node, stack):
        got = matmul(pick_ref[node - 64], stack)
        kept_ref[pl.ds(node * KEPT, 64), :] = got
        level_ref[node - 64] = got.astype(BF16)

    def first_levels(low_ref, high_ref):
        for j in range(32):
            pair = [low_ref[2 * j], high_ref[2 * j], low_ref[2 * j + 1], high_ref[2 * j + 1]]
            select(64 + j, jnp.concatenate(pair, 0))
        for chip in range(64):
            kept_ref[pl.ds(chip * KEPT, 32), :] = low_ref[chip].astype(F32)
            kept_ref[pl.ds(chip * KEPT + 32, 32), :] = high_ref[chip].astype(F32)

    @pl.when(where_ref[0] % 2 == 0)
    def _():
        first_levels(mine_ref, other_ref)

    @pl.when(where_ref[0] % 2 == 1)
    def _():
        first_levels(other_ref, mine_ref)

    before, offset, count = 64, 96, 16
    while count >= 1:
        for j in range(count):
            select(offset + j, level_ref[pl.ds(before + 2 * j - 64, 2)].reshape(128, 128))
        before, offset, count = offset, offset + count, count // 2

    def put(at):
        span = pl.ds(at, 16)
        return pltpu.make_async_copy(out_ref.at[span], out_hbm.at[span], sem.at[at // 16])

    for slot in range(64):
        turned = jnp.transpose(kept_ref[pl.ds(slot, 128, stride=KEPT), :])
        out_ref[slot] = (turned[:64] + turned[64:])[:, :127]
        if slot % 16 == 15:
            put(slot - 15).start()
    for at in range(0, 64, 16):
        put(at).wait()


def middle_call(*operands):
    return pl.pallas_call(
        middle_kernel,
        in_specs=[whole((4096, 128)), whole((256, 128)), whole(FLAT), whole(SIDE), whole(SIDE), whole(SIDE)],
        out_specs=[whole((4096, 128)), whole(FLAT)],
        out_shape=[jax.ShapeDtypeStruct((4096, 128), F32), jax.ShapeDtypeStruct(FLAT, F32)],
        scratch_shapes=[pltpu.VMEM(FLAT, F32), pltpu.VMEM((512, 128), F32)],
        compiler_params=LIMIT,
    )(*operands)


def outer_rows_call(*operands):
    rows = jax.ShapeDtypeStruct((32, 128), F32)
    return pl.pallas_call(
        outer_rows_kernel,
        in_specs=[whole(FLAT), whole((256, 128)), whole(FLAT)] + [whole(EDGE)] * 4,
        out_specs=[whole((32, 128)), whole((32, 128)), whole((1024, 128))],
        out_shape=[rows, rows, jax.ShapeDtypeStruct((1024, 128), F32)],
        scratch_shapes=[pltpu.VMEM((512, 128), F32)],
        compiler_params=LIMIT,
    )(*operands)


def outer_flux_call(*operands):
    return pl.pallas_call(
        outer_flux_kernel,
        in_specs=[whole((4096, 128)), whole((1024, 128))],
        out_specs=HBM,
        out_shape=jax.ShapeDtypeStruct((64, 8, 8, 128), BF16),
        scratch_shapes=[
            pltpu.VMEM((64, 8, 8, 128), BF16),
            pltpu.VMEM((1024, 128), F32),
            pltpu.SemaphoreType.DMA((2,)),
        ],
        compiler_params=LIMIT,
    )(*operands)


def tree_call(*operands):
    return pl.pallas_call(
        tree_kernel,
        in_specs=[SMEM, whole((63, 64, 128)), whole((64, 32, 128)), whole((64, 32, 128))],
        out_specs=HBM,
        out_shape=jax.ShapeDtypeStruct((64, 64, 127), F32),
        scratch_shapes=[
            pltpu.VMEM((63, 64, 128), BF16),
            pltpu.VMEM((128 * KEPT, 128), F32),
            pltpu.VMEM((64, 64, 127), F32),
            pltpu.SemaphoreType.DMA((4,)),
        ],
        compiler_params=LIMIT,
    )(*operands)


def local(states, class_map, perm_table, candidates, merge_order):
    tile = lax.axis_index("gx") * lax.axis_size("gy") + lax.axis_index("gy")
    where = tile.reshape(1).astype(jnp.int32)
    states, class_map, perm_table, candidates, merge_rows = (
        pltpu.with_memory_space_constraint(value, pltpu.HBM)
        for value in (states, class_map, perm_table, candidates.reshape(128, 64), merge_order)
    )
    states_shape = (2, 64, 8, 8, 128)
    read_scratch = [pltpu.VMEM(CUBE, jnp.int32), pltpu.SMEM((8,), F32)]
    low, high = pl.pallas_call(
        edge_x_kernel,
        in_specs=[HBM, HBM, HBM],
        out_specs=[whole(EDGE), whole(EDGE)],
        out_shape=[jax.ShapeDtypeStruct(EDGE, BF16), jax.ShapeDtypeStruct(EDGE, BF16)],
        scratch_shapes=[pltpu.VMEM(states_shape, BF16)]
        + read_scratch
        + [pltpu.VMEM((129 * 64, 128), F32), pltpu.SemaphoreType.DMA((4,))],
        compiler_params=LIMIT,
    )(perm_table, class_map, states)

    def shift(value, axis, by):
        count = lax.axis_size(axis)
        return lax.ppermute(value, axis, [(i, (i + by) % count) for i in range(count)])

    from_low = shift(high, "gx", 1)
    from_high = shift(low, "gx", -1)

    side, perm, near_states, cells, hits = pl.pallas_call(
        edge_y_kernel,
        in_specs=[SMEM] + [HBM] * 5,
        out_specs=[whole(SIDE), whole(CUBE), whole(states_shape), whole((256, 128)), whole(FLAT)],
        out_shape=[
            jax.ShapeDtypeStruct(SIDE, BF16),
            jax.ShapeDtypeStruct(CUBE, F32),
            jax.ShapeDtypeStruct(states_shape, BF16),
            jax.ShapeDtypeStruct((256, 128), BF16),
            jax.ShapeDtypeStruct(FLAT, F32),
        ],
        scratch_shapes=[
            pltpu.VMEM(CUBE, jnp.int32),
            pltpu.VMEM((1, 64), jnp.int32),
            pltpu.VMEM((1, 128), jnp.int32),
            pltpu.SMEM((8,), F32),
            pltpu.SemaphoreType.DMA((6,)),
        ],
        compiler_params=LIMIT,
    )(where, perm_table, class_map, candidates, merge_rows, states)
    side_low = shift(side, "gy", 1)
    side_high = shift(side, "gy", -1)

    inner = pl.pallas_call(
        inner_kernel,
        in_specs=[whole(CUBE), whole(states_shape)],
        out_specs=whole((4096, 128)),
        out_shape=jax.ShapeDtypeStruct((4096, 128), F32),
        scratch_shapes=[
            pltpu.VMEM(CUBE, F32),
            pltpu.VMEM(FLAT, F32),
            pltpu.VMEM((7, 8, 128), F32),
            pltpu.VMEM((128, 128), BF16),
        ],
        compiler_params=LIMIT,
    )(perm, near_states)
    numbers = lax.broadcasted_iota(jnp.int32, (63, 64, 128), 2)
    picks = (merge_order[64:, :64, None] == numbers).astype(BF16)
    inner, picks = lax.optimization_barrier((inner, picks))

    within, part_rows = middle_call(inner, cells, hits, side, side_low, side_high)
    mine_rows, send_rows, q_x = outer_rows_call(part_rows, cells, hits, low, high, from_low, from_high)

    swap = [(i, i ^ 1) for i in range(8)]
    got_rows = lax.ppermute(send_rows, "gy", swap)
    flux = outer_flux_call(within, q_x)
    flux, got_rows = lax.optimization_barrier((flux, got_rows))
    merged = mine_rows[:, :64] + got_rows[:, :64]
    top = merged.astype(BF16)
    rest = (merged - lax.reduce_precision(merged, 8, 7)).astype(BF16)
    spread = jnp.broadcast_to(jnp.concatenate([top, rest], 1)[None], (64, 32, 128))
    peers = [[i * 8 + j * 2 + c for i in range(16) for j in range(4)] for c in range(2)]
    mine = lax.all_to_all(spread, ("gx", "gy"), 0, 0, axis_index_groups=peers)
    other = lax.ppermute(mine, "gy", swap)

    kept = tree_call(where, picks, mine, other)
    return flux, jnp.transpose(kept, (2, 0, 1))


def solution(mesh):
    in_specs = (P(None, None, None, "gx", "gy"), P(None, "gx", "gy"), P(), P(), P())
    out_specs = (P(None, None, "gx", "gy"), P())
    return jax.shard_map(local, mesh=mesh, in_specs=in_specs, out_specs=out_specs, check_vma=False)
```
